512 devices in a mesh: seq: 64 (over z, x), head: 8 (over y, core).
Axes of the slice: x: 4, y: 4, z: 16, core: 2. Of those that a mesh axis runs over, the one named last changes fastest.
Arguments:
- head_inputs: bfloat16 [8192, 8192], P(('seq', 'head')), may hold values from -1.5 to 1.5
- state_proj: bfloat16 [8192, 2048], P(('seq', 'head')), may hold values from -6 to 6
- gate_inputs: bfloat16 [8192, 8192], P(('seq', 'head')), may hold values from -6 to 6
- step_raw: bfloat16 [8192, 128], P(('seq', 'head')), may hold values from -4 to 4
- step_bias: float32 [128], P('head'), may hold values from -2 to 2
- decay_log: float32 [128], P('head'), may hold values from -13 to -2
- skip_gain: float32 [128], P('head'), may hold values from 0.5 to 1.5
- filter_inner: float32 [4, 8192], P(None, 'head'), may hold values from -3 to 3
- filter_state: float32 [4, 2048], P(None, 'head'), may hold values from -3 to 3
- norm_gain: float32 [8192], P('head'), may hold values from 0.5 to 1.5
- prompt_lengths: int32 [7], replicated, may hold values from 1 to 4096, 8192 in all
- request_prompt: int32 [64, 1], P('seq'), may hold values from 0 to 6
Outputs:
- hidden: bfloat16 [8192, 8192], P('seq', 'head')
- final_state: float32 [64, 128, 64, 128], P('seq', 'head')
- edge_inner: bfloat16 [64, 3, 8192], P('seq', None, 'head')
- edge_state: bfloat16 [64, 3, 2048], P('seq', None, 'head')
The draws below stay inside these ranges and needn't reach their ends.
Inputs may be any that keep to these rules, and one draw needn't show every extreme that they name: `request_prompt`: every prompt is shared by at least one request; request r is served by index r of seq.
All inputs are finite; a program needn't handle non-finite values.
Results may differ from the reference program's by a relative error of at most 0.0065.
Values may be sent and summed in bfloat16 or wider, within the bound.
No kernel may reach another device: no remote copies, remote signals or barrier semaphores. Data moves between devices by JAX's collectives and lax.ppermute only.
A program may use at most 128 MiB of HBM per device.

```python
import math
import jax
import jax.numpy as jnp
import numpy as np
from jax import lax

HEADS = 128
HEAD_DIM = 64
GROUPS = 8
STATE = 128
CONV = 4
SPAN = 256
INNER = 8192
PROJ = 2048
TOK_DEV = 128
TOKENS = 8192
PROMPTS = 7
MAX_LEN = 4096
REQUESTS = 64


def draw_decay_log(key, part):
    pick_key = jax.random.fold_in(key, 11)
    spread_key = jax.random.fold_in(key, 23)
    spread = jax.random.uniform(spread_key, (HEADS,), jnp.float32)
    slow = jax.random.uniform(pick_key, (HEADS,), jnp.float32) < 0.5
    slow_rate = jnp.log(0.2 / TOKENS) + spread * jnp.log(5.0)
    fast_rate = jnp.log(0.02) + spread * jnp.log(5.0)
    return jnp.where(slow, slow_rate, fast_rate).astype(jnp.float32)


def level_of(rng, shape, pieces, least, top_value):
    gain, own = 1.0, jax.random.fold_in(rng, 6)
    for axis_at, shards_of in pieces:
        heights = jnp.exp(jax.random.uniform(jax.random.fold_in(own, axis_at), (shards_of,), jnp.float32, least / len(pieces), top_value / len(pieces)))
        gain = gain * jnp.repeat(heights, shape[axis_at] // shards_of).reshape([-1 if axis == axis_at else 1 for axis in range(len(shape))])
    return gain


def different_ones(own_key, rows, number_of, top, lift):
    order = jax.random.permutation(jax.random.fold_in(own_key, 1), number_of)
    favour = order
    for power in range(3):
        favour = favour * favour // number_of
    favour = favour * lift // number_of
    tickets = jax.random.randint(jax.random.fold_in(own_key, 2), (rows, number_of), 0, 4096) + favour
    sure = jax.random.permutation(jax.random.fold_in(own_key, 3), rows)[jnp.arange(number_of) % rows]
    tickets = jnp.where(jnp.arange(rows)[:, None] == sure[None, :], 1 << 14, tickets)
    score = tickets * number_of + jnp.arange(number_of)
    return lax.top_k(score.astype(jnp.int32), top)[1].astype(jnp.int32)


def split_up(amount, total, limit, skew):
    loads = [(1 << 20) // math.isqrt(standing ** skew) + 1 for standing in range(2, amount + 1)]
    rest, given = total - limit - (amount - 1), [1] * (amount - 1)
    while rest > 0:
        candidates = [i for i in range(amount - 1) if given[i] < limit]
        mass, remaining = sum([loads[i] for i in candidates]), rest
        for i in candidates:
            more = min(limit - given[i], max(1, remaining * loads[i] // mass), rest)
            given[i] = given[i] + more
            rest = rest - more
    return np.array([limit] + given)


def ragged(stream_key, amount, total, bound, lean):
    if amount == 2:
        one = jax.random.randint(stream_key, (), max(1, total - bound), min(bound, total - 1) + 1)
        return jnp.stack([one, total - one])
    lengths = jnp.asarray(split_up(amount, total, bound, lean), jnp.int32)
    twos = (amount - 1) // 2
    donor, receiver = lengths[1:1 + 2 * twos:2], lengths[2:2 + 2 * twos:2]
    slack = jnp.minimum(donor - 1, bound - receiver)
    shifted = jax.random.randint(jax.random.fold_in(stream_key, 1), (twos,), 0, 1 << 20) % (slack + 1)
    lengths = lengths.at[1:1 + 2 * twos:2].set(donor - shifted).at[2:2 + 2 * twos:2].set(receiver + shifted)
    return lengths[jax.random.permutation(jax.random.fold_in(stream_key, 2), amount)]


def centred(rng, shape, deviation, most, pieces=(), kind=jnp.bfloat16):
    values = deviation * jax.random.normal(rng, shape, jnp.float32)
    if pieces:
        values = values * level_of(rng, shape, pieces, -0.22, 0.18)
    return jnp.clip(values, -most, most).astype(kind)


def setup_inputs(seed: int = 0) -> dict:
    key_of = jax.random.split(jax.random.key(seed), 13)
    head_inputs = centred(key_of[0], (TOKENS, INNER), 0.25, 1.5, ((0, 512),))
    state_proj = centred(key_of[1], (TOKENS, PROJ), 1.0, 6.0, ((0, 512),))
    gate_inputs = centred(key_of[2], (TOKENS, INNER), 1.0, 6.0, ((0, 512),))
    step_raw = centred(key_of[3], (TOKENS, HEADS), 1.0, 4.0, ((0, 512),))
    step_bias = centred(key_of[4], (HEADS,), 0.5, 2.0, ((0, 8),), jnp.float32)
    decay_log = draw_decay_log(jax.random.fold_in(key_of[12], 71), 0)
    skip_gain = jnp.clip(0.5 + 1.0 * jax.random.uniform(key_of[6], (HEADS,), jnp.float32) ** level_of(key_of[6], (HEADS,), ((0, 8),), -0.2, 0.2), 0.5, 1.5)
    filter_inner = centred(key_of[7], (CONV, INNER), CONV ** -0.5, 3.0, ((1, 8),), jnp.float32)
    filter_state = centred(key_of[8], (CONV, PROJ), CONV ** -0.5, 3.0, ((1, 8),), jnp.float32)
    norm_gain = jnp.clip(1.0 + 0.1 * jax.random.normal(key_of[9], (INNER,), jnp.float32), 0.5, 1.5)
    prompt_lengths = ragged(key_of[10], PROMPTS, TOKENS, MAX_LEN, 2).astype(jnp.int32)
    request_prompt = different_ones(key_of[11], REQUESTS, PROMPTS, 1, 0)
    return {"head_inputs": head_inputs, "state_proj": state_proj, "gate_inputs": gate_inputs, "step_raw": step_raw, "step_bias": step_bias, "decay_log": decay_log, "skip_gain": skip_gain, "filter_inner": filter_inner, "filter_state": filter_state, "norm_gain": norm_gain, "prompt_lengths": prompt_lengths, "request_prompt": request_prompt}


EPSILON = 1e-05

def segment_of(position, prompt_starts):
    return (lax.optimization_barrier(jnp.sum((position[:, None] >= prompt_starts[None, :]).astype(jnp.int32), axis=1)) - 1).astype(jnp.int32)

def start_of(position, prompt_starts):
    return lax.optimization_barrier(jnp.max(jnp.where(position[:, None] >= prompt_starts[None, :], prompt_starts[None, :], 0), axis=1)).astype(jnp.int32)

def causal_filter(source_rows, prior_rows, kernel, position, row_start):
    padded = jnp.concatenate([prior_rows, source_rows], axis=0)
    row_count = source_rows.shape[0]
    summed = jnp.zeros(source_rows.shape, jnp.float32)
    for offset in range(CONV):
        source = position - (CONV - 1) + offset
        inside = (source >= row_start).astype(jnp.float32)[:, None]
        summed = summed + inside * padded[offset:offset + row_count].astype(jnp.float32) * kernel[offset][None, :]
    return jax.nn.silu(summed).astype(jnp.bfloat16)

def reference(head_inputs, state_proj, gate_inputs, step_raw, step_bias, decay_log, skip_gain, filter_inner, filter_state, norm_gain, prompt_lengths, request_prompt):
    block_len = min(TOK_DEV, SPAN)
    prompt_ends = (jnp.cumsum(prompt_lengths) - 1).astype(jnp.int32)
    prompt_starts = (prompt_ends + 1 - prompt_lengths).astype(jnp.int32)
    prompt_ids = jnp.arange(PROMPTS, dtype=jnp.int32)
    per_group = HEADS // GROUPS
    edge_rows = CONV - 1
    span_count = TOKENS // block_len
    decay_rate = -jnp.exp(decay_log)

    def span_step(running, inputs):
        state, left_inner, left_state, finals, edge_inner, edge_state = running
        span_index, inner_rows, proj_rows, gate_rows, step_rows = inputs
        first_row = (span_index * block_len).astype(jnp.int32)
        position = (first_row + jnp.arange(block_len, dtype=jnp.int32)).astype(jnp.int32)
        segment = segment_of(position, prompt_starts)
        row_start = start_of(position, prompt_starts)
        prior_segment = segment_of(jnp.reshape(first_row - 1, (1,)).astype(jnp.int32), prompt_starts)[0]
        inner_act = causal_filter(inner_rows, left_inner, filter_inner, position, row_start)
        state_act = causal_filter(proj_rows, left_state, filter_state, position, row_start)
        proj_pairs = state_act.reshape(block_len, GROUPS, 2, STATE).astype(jnp.float32)
        write_proj = proj_pairs[:, :, 0]
        read_proj = proj_pairs[:, :, 1]
        step_size = jax.nn.softplus(step_rows.astype(jnp.float32) + step_bias[None, :])
        log_decay = jnp.cumsum(step_size * decay_rate[None, :], axis=0)
        causal_mask = (segment[:, None] == segment[None, :]) & (position[:, None] >= position[None, :])
        decay_heads = log_decay.T
        log_gap = jnp.where(causal_mask[None], decay_heads[:, :, None] - decay_heads[:, None, :], -jnp.inf)
        scores = jnp.einsum('tgs,jgs->gtj', read_proj, write_proj)
        scores = jnp.repeat(scores, per_group, axis=0)
        mixing = (scores * jnp.exp(log_gap) * step_size.T[:, None, :]).astype(jnp.bfloat16)
        head_act = inner_act.reshape(block_len, HEADS, HEAD_DIM).astype(jnp.float32)
        within = jnp.einsum('htj,jhp->thp', mixing.astype(jnp.float32), head_act)
        inflow = jnp.exp(log_decay) * (segment == prior_segment).astype(jnp.float32)[:, None]
        across = jnp.einsum('tgs,gkps->tgkp', read_proj, state, precision=lax.Precision.HIGHEST).reshape(block_len, HEADS, HEAD_DIM)
        output_sum = within + inflow[:, :, None] * across + skip_gain[None, :, None] * head_act
        gated = output_sum.reshape(block_len, INNER) * jax.nn.silu(gate_rows.astype(jnp.float32))
        grouped = gated.reshape(block_len, GROUPS, INNER // GROUPS)
        inverse_rms = lax.rsqrt(lax.optimization_barrier(jnp.mean(grouped * grouped, axis=2, keepdims=True)) + EPSILON)
        hidden = ((grouped * inverse_rms).reshape(block_len, INNER) * norm_gain[None, :]).astype(jnp.bfloat16)
        ends_here = (prompt_ends >= first_row) & (prompt_ends < first_row + block_len)
        end_onehot = (position[None, :] == prompt_ends[:, None]).astype(jnp.float32)
        end_decay = jnp.dot(end_onehot, log_decay, precision=lax.Precision.HIGHEST)
        member = (segment[None, :] == prompt_ids[:, None]) & (position[None, :] <= prompt_ends[:, None]) & ends_here[:, None]
        decay_gap = jnp.where(member[:, :, None], end_decay[:, None, :] - log_decay[None], -jnp.inf)
        weighted = ((jnp.exp(decay_gap) * step_size[None])[..., None] * head_act[None]).astype(jnp.bfloat16)
        own_part = jnp.einsum('ptgkd,tgs->pgkds', weighted.astype(jnp.float32).reshape(PROMPTS, block_len, GROUPS, per_group, HEAD_DIM), write_proj)
        carried = jnp.exp(end_decay) * (ends_here & (prompt_ids == prior_segment)).astype(jnp.float32)[:, None]
        finals = finals + own_part + carried.reshape(PROMPTS, GROUPS, per_group)[..., None, None] * state[None]
        offsets = prompt_ends[:, None] - (edge_rows - 1) + jnp.arange(edge_rows, dtype=jnp.int32)[None, :]
        index_rows = jnp.clip(offsets - (first_row - edge_rows), 0, block_len + edge_rows - 1).astype(jnp.int32)
        inside = ((offsets >= prompt_starts[:, None]) & ends_here[:, None])[..., None]
        padded_inner = jnp.concatenate([left_inner, inner_rows], axis=0)
        padded_state = jnp.concatenate([left_state, proj_rows], axis=0)
        edge_inner = edge_inner + jnp.where(inside, padded_inner[index_rows], 0).astype(jnp.float32)
        edge_state = edge_state + jnp.where(inside, padded_state[index_rows], 0).astype(jnp.float32)
        segment_last = segment[block_len - 1]
        tail_mask = segment == segment_last
        tail_gap = jnp.where(tail_mask[:, None], log_decay[block_len - 1][None, :] - log_decay, -jnp.inf)
        tail_weighted = ((jnp.exp(tail_gap) * step_size)[..., None] * head_act).astype(jnp.bfloat16)
        block_state = jnp.einsum('tgkd,tgs->gkds', tail_weighted.astype(jnp.float32).reshape(block_len, GROUPS, per_group, HEAD_DIM), write_proj)
        keep_last = jnp.exp(log_decay[block_len - 1]) * (segment_last == prior_segment).astype(jnp.float32)
        state = keep_last.reshape(GROUPS, per_group)[..., None, None] * state + block_state
        left_inner = inner_rows[block_len - edge_rows:]
        left_state = proj_rows[block_len - edge_rows:]
        return ((state, left_inner, left_state, finals, edge_inner, edge_state), hidden)
    initial = (jnp.zeros((GROUPS, per_group, HEAD_DIM, STATE), jnp.float32), jnp.zeros((edge_rows, INNER), jnp.bfloat16), jnp.zeros((edge_rows, PROJ), jnp.bfloat16), jnp.zeros((PROMPTS, GROUPS, per_group, HEAD_DIM, STATE), jnp.float32), jnp.zeros((PROMPTS, edge_rows, INNER), jnp.float32), jnp.zeros((PROMPTS, edge_rows, PROJ), jnp.float32))
    inputs = (jnp.arange(span_count, dtype=jnp.int32), head_inputs.reshape(span_count, block_len, INNER), state_proj.reshape(span_count, block_len, PROJ), gate_inputs.reshape(span_count, block_len, INNER), step_raw.reshape(span_count, block_len, HEADS))
    final_running, hidden = lax.scan(span_step, initial, inputs)
    finals = final_running[3].reshape(PROMPTS, HEADS, HEAD_DIM, STATE)
    chosen = request_prompt[:, 0].astype(jnp.int32)
    final_state = finals[chosen]
    edge_inner = final_running[4][chosen].astype(jnp.bfloat16)
    edge_state = final_running[5][chosen].astype(jnp.bfloat16)
    return (hidden.reshape(TOKENS, INNER), final_state, edge_inner, edge_state)
```

```python
import functools

import jax
import jax.numpy as jnp
from jax import lax
from jax.experimental import pallas as pl
from jax.experimental.pallas import tpu as pltpu
from jax.sharding import PartitionSpec as P

STATE = 128
EPSILON = 1e-05
PROMPTS = 7
ROWS = 128
WIDTH = 1024
WIDE = 1280
HEAD = 64
BIG = 1 << 30
F32 = jnp.float32
BF16 = jnp.bfloat16

MESSAGE = 40


def dot(a, b, dims, precision=None):
    return lax.dot_general(a, b, (dims, ((), ())), precision=precision, preferred_element_type=F32)


def bounds(length_ref):
    starts, ends = [], []
    total = jnp.int32(0)
    for p in range(PROMPTS):
        starts.append(total)
        total = total + length_ref[p]
        ends.append(total - 1)
    return starts, ends


def segment_at(position, starts):
    found = jnp.zeros_like(position) - 1
    for start in starts:
        found = found + (position >= start).astype(jnp.int32)
    return found


def spread(weights, tile, lane):
    left = jnp.broadcast_to(weights[:, 2 * tile : 2 * tile + 1], lane.shape)
    right = jnp.broadcast_to(weights[:, 2 * tile + 1 : 2 * tile + 2], lane.shape)
    return jnp.where(lane < HEAD, left, right)


def parts(value):
    first = value.astype(BF16).astype(F32)
    rest = value - first
    second = rest.astype(BF16).astype(F32)
    return first, second, rest - second


def pack_kernel(inner_ref, proj_ref, step_ref, out_ref):
    for k in range(out_ref.shape[0]):
        out_ref[k, :, 0:WIDTH] = inner_ref[:, k * WIDTH : (k + 1) * WIDTH]
        out_ref[k, :, WIDTH:WIDE] = proj_ref[:, k * 256 : (k + 1) * 256]
        out_ref[k, :, WIDE : WIDE + 128] = step_ref[...]


def front_kernel(
    place_ref, length_ref, request_ref, rows_ref, halo_ref, taps_ref, head_ref,
    message_ref, act_ref, decay_ref, step_ref, padded,
):
    first = place_ref[0] * ROWS
    starts, ends = bounds(length_ref)
    lane = lax.broadcasted_iota(jnp.int32, (ROWS, 128), 1)
    position = lax.broadcasted_iota(jnp.int32, (ROWS, 128), 0) + first
    segment = segment_at(position, starts)
    row_start = jnp.zeros_like(position)
    for start in starts:
        row_start = jnp.where(position >= start, start, row_start)
    before = segment_at(first - 1, starts)
    last = segment_at(first + ROWS - 1, starts)
    end, end_prompt, end_start = jnp.int32(BIG), jnp.int32(-2), jnp.int32(0)
    for p in reversed(range(PROMPTS)):
        here = (ends[p] >= first) & (ends[p] < first + ROWS)
        end = jnp.where(here, ends[p], end)
        end_prompt = jnp.where(here, p, end_prompt)
        end_start = jnp.where(here, starts[p], end_start)
    some_end = end < BIG

    padded[0:8, :] = halo_ref[...].astype(F32)
    padded[8:, :] = rows_ref[:, 0:WIDE].astype(F32)
    inside = [(position - 3 + k) >= row_start for k in range(4)]
    for tile in range(WIDE // 128):
        cols = slice(tile * 128, (tile + 1) * 128)
        total = jnp.zeros((ROWS, 128), F32)
        for k in range(4):
            total = total + jnp.where(inside[k], padded[5 + k : 5 + k + ROWS, cols], 0.0) * taps_ref[k : k + 1, cols]
        act_ref[:, cols] = (total * jax.nn.sigmoid(total)).astype(BF16)

    raw = rows_ref[:, WIDE : WIDE + 128].astype(F32)
    raw = pltpu.roll(raw, place_ref[2], 1)
    step = jax.nn.softplus(raw + head_ref[0:1, :])
    rate = step * -jnp.exp(head_ref[1:2, :])
    lower = (
        lax.broadcasted_iota(jnp.int32, (ROWS, ROWS), 0) >= lax.broadcasted_iota(jnp.int32, (ROWS, ROWS), 1)
    ).astype(F32)
    decay = dot(lower, rate, ((1,), (0,)), lax.Precision.HIGHEST)
    decay_ref[...] = decay
    step_ref[...] = step

    last_decay = decay[ROWS - 1 : ROWS, :]
    tail = jnp.where(segment == last, jnp.exp(jnp.minimum(last_decay - decay, 0.0)), 0.0) * step
    end_decay = jnp.sum(jnp.where(position == end, decay, 0.0), axis=0, keepdims=True)
    member = (segment == end_prompt) & (position <= end)
    own = jnp.where(member, jnp.exp(jnp.minimum(end_decay - decay, 0.0)), 0.0) * step
    write = act_ref[:, WIDTH : WIDTH + STATE]
    for tile in range(WIDTH // 128):
        x = act_ref[:, tile * 128 : (tile + 1) * 128].astype(F32)
        for at, weights in ((0, tail), (16, own)):
            weighted = (spread(weights, tile, lane) * x).astype(BF16)
            block = dot(weighted, write, ((0,), (0,)))
            message_ref[tile * 8 : (tile + 1) * 8, at : at + 16, :] = block.astype(BF16).reshape(8, 16, 128)

    keep = jnp.where(last == before, jnp.exp(last_decay), 0.0)
    carried = jnp.where(some_end & (end_prompt == before), jnp.exp(end_decay), 0.0)
    index = lax.broadcasted_iota(jnp.int32, (8, 128), 0)
    small = jnp.where(index == 7, request_ref[0, 0].astype(F32), jnp.zeros((8, 128), F32))
    for at, piece in enumerate(parts(keep) + parts(carried)):
        small = jnp.where(index == at + 1, piece, small)
    for k in range(3):
        local = jnp.where(some_end, end - first, 0) - 2 + k
        valid = some_end & (end - 2 + k >= end_start)
        row = jnp.where(valid, padded[pl.ds(8 + local, 1), :], 0.0)
        for c in range(WIDE // 128):
            piece = row[:, c * 128 : (c + 1) * 128]
            message_ref[k * 10 + c, 32:40, :] = jnp.where(index == 0, piece, small).astype(BF16)
    rest = small.astype(BF16)
    for k in range(30, 64):
        message_ref[k, 32:40, :] = rest


def scan_kernel(place_ref, length_ref, got_ref, extra_ref, out_ref, states, finals):
    starts, ends = bounds(length_ref)
    head = place_ref[0] // 4
    pick = (lax.broadcasted_iota(jnp.int32, (128, 128), 0) == head).astype(BF16)
    small = dot(got_ref[:, 32:40, :].reshape(64 * 8, 128), pick, ((1,), (0,)))
    state = jnp.zeros((16, 128), F32)
    for j in range(64):
        states[j, 0:16, :] = state
        keep = small[8 * j + 1 : 8 * j + 2] + small[8 * j + 2 : 8 * j + 3] + small[8 * j + 3 : 8 * j + 4]
        states[j, 16:17, :] = small[8 * j + 4 : 8 * j + 5] + small[8 * j + 5 : 8 * j + 6] + small[8 * j + 6 : 8 * j + 7]
        out_ref[j, 0:16, :] = state.astype(BF16)
        state = keep * state + got_ref[j, 0:16, :].astype(F32)
    for p in range(PROMPTS):
        block = ends[p] // ROWS
        one = got_ref[block, 16:40, :].astype(F32)
        value = one[0:16] + states[block, 16:17, :] * states[block, 0:16, :]
        value = jnp.concatenate([value, one[16:24]], axis=0)
        if p:
            value = jnp.where(ends[p - 1] // ROWS == block, extra_ref[p], value)
        finals[p] = value
    for r in range(64):
        request = got_ref[r, 39:40, :].astype(F32)
        value = finals[0]
        for p in range(1, PROMPTS):
            value = jnp.where(request == float(p), finals[p], value)
        out_ref[r, 16:40, :] = value.astype(BF16)


def within_kernel(place_ref, length_ref, act_ref, decay_ref, step_ref, gate_ref, head_ref, own_ref, in_ref):
    first = place_ref[0] * ROWS
    starts, _ = bounds(length_ref)
    before = segment_at(first - 1, starts)
    lane = lax.broadcasted_iota(jnp.int32, (ROWS, 128), 1)
    sub = lax.broadcasted_iota(jnp.int32, (ROWS, 128), 0)
    segment = segment_at(sub + first, starts)
    segment_j = segment_at(lane + first, starts)
    causal = (segment == segment_j) & (sub >= lane)
    write = act_ref[:, WIDTH : WIDTH + STATE]
    read = act_ref[:, WIDTH + STATE : WIDE]
    scores = dot(read, write, ((1,), (1,)))
    decay = decay_ref[...]
    decay_t = decay.T
    step_t = step_ref[...].T
    inflow = jnp.where(segment == before, jnp.exp(decay), 0.0)
    for tile in range(WIDTH // 128):
        cols = slice(tile * 128, (tile + 1) * 128)
        x = act_ref[:, cols]
        mixing = []
        for head in (2 * tile, 2 * tile + 1):
            gap = decay[:, head : head + 1] - decay_t[head : head + 1, :]
            weight = jnp.exp(jnp.where(causal, gap, -jnp.inf))
            mixing.append((scores * weight * step_t[head : head + 1, :]).astype(BF16))
        none = jnp.zeros_like(x)
        both = jnp.concatenate([jnp.where(lane < HEAD, x, none), jnp.where(lane < HEAD, none, x)], axis=0)
        within = dot(jnp.concatenate(mixing, axis=1), both, ((1,), (0,)))
        within = within + head_ref[2 + tile : 3 + tile, :] * x.astype(F32)
        gate = gate_ref[:, cols].astype(F32)
        gate = gate * jax.nn.sigmoid(gate)
        own_ref[:, cols] = within * gate
        in_ref[:, cols] = spread(inflow, tile, lane) * gate


def back_kernel(act_ref, own_ref, in_ref, got_ref, gain_ref, hidden_ref, final_ref, inner_ref, proj_ref, gated):
    read = act_ref[:, WIDTH + STATE : WIDE]
    total = jnp.zeros((ROWS, 128), F32)
    for tile in range(WIDTH // 128):
        cols = slice(tile * 128, (tile + 1) * 128)
        state = got_ref[tile * 8 : (tile + 1) * 8, 0:16, :].reshape(128, 128)
        across = dot(read, state, ((1,), (1,)))
        value = own_ref[:, cols] + in_ref[:, cols] * across
        gated[:, cols] = value
        total = total + value * value
    mean = jnp.sum(total, axis=1, keepdims=True) * (1.0 / WIDTH)
    inverse = lax.rsqrt(mean + EPSILON)
    for tile in range(WIDTH // 128):
        cols = slice(tile * 128, (tile + 1) * 128)
        hidden_ref[:, cols] = ((gated[:, cols] * inverse) * gain_ref[:, cols]).astype(BF16)
        final_ref[tile * 128 : (tile + 1) * 128, :] = (
            got_ref[tile * 8 : (tile + 1) * 8, 16:32, :].reshape(128, 128).astype(F32)
        )
    for k in range(3):
        for c in range(8):
            inner_ref[0, k : k + 1, c * 128 : (c + 1) * 128] = got_ref[k * 10 + c, 32:33, :]
        for c in range(2):
            proj_ref[0, k : k + 1, c * 128 : (c + 1) * 128] = got_ref[k * 10 + 8 + c, 32:33, :]


def call(kernel, ins, outs, scratch=(), scalars=0):
    smem = pl.BlockSpec(memory_space=pltpu.SMEM)
    vmem = pl.BlockSpec(memory_space=pltpu.VMEM)
    return pl.pallas_call(
        kernel,
        out_shape=outs,
        in_specs=[smem] * scalars + [vmem] * (len(ins) - scalars),
        out_specs=jax.tree.map(lambda _: vmem, outs),
        scratch_shapes=list(scratch),
    )(*ins)


def later_ends(place, prompt_lengths, rows, halo, act, decay, step):
    ends = jnp.cumsum(prompt_lengths) - 1
    starts = ends + 1 - prompt_lengths
    ids = jnp.arange(PROMPTS, dtype=jnp.int32)
    block = ends // ROWS
    rank = jnp.sum((block[None, :] == block[:, None]) & (ids[None, :] < ids[:, None]), axis=1)
    position = place * ROWS + jnp.arange(ROWS, dtype=jnp.int32)

    def step_of(carry):
        k, extra = carry
        mine = (block == place) & (rank == k)
        some = jnp.any(mine)
        end = jnp.sum(jnp.where(mine, ends, 0))
        start = jnp.sum(jnp.where(mine, starts, 0))
        member = some & (position >= start) & (position <= end)
        end_decay = jnp.sum(jnp.where((position == end)[:, None], decay, 0.0), axis=0, keepdims=True)
        weights = jnp.where(member[:, None], jnp.exp(jnp.minimum(end_decay - decay, 0.0)), 0.0) * step
        weights = weights[:, : WIDTH // HEAD]
        x = act[:, :WIDTH].reshape(ROWS, -1, HEAD).astype(F32)
        weighted = (weights[:, :, None] * x).reshape(ROWS, WIDTH).astype(BF16)
        own = dot(weighted, act[:, WIDTH : WIDTH + STATE], ((0,), (0,))).astype(BF16)
        padded = jnp.concatenate([halo, rows[:, :WIDE]], axis=0)
        wanted = end - 2 + jnp.arange(3, dtype=jnp.int32)
        onehot = (jnp.arange(ROWS + 8)[None, :] + (place * ROWS - 8) == wanted[:, None]) & some
        onehot = onehot & (wanted >= start)[:, None]
        edge = dot(onehot.astype(BF16), padded, ((1,), (0,))).astype(BF16)
        edge = jnp.pad(edge.reshape(30, 1, 128), ((0, 34), (0, 7), (0, 0)))
        sent = jnp.concatenate([own.reshape(64, 16, 128), edge], axis=1)
        got = lax.all_to_all(sent, "seq", 0, 0)
        taken = got[block].astype(F32)
        return k + 1, jnp.where((rank == k)[:, None, None], taken, extra)

    most = jnp.max(rank)
    return lax.while_loop(
        lambda carry: carry[0] <= most,
        step_of,
        (jnp.ones_like(most), jnp.zeros((PROMPTS, 24, 128), F32)),
    )[1]


def per_device(
    head_inputs,
    state_proj,
    gate_inputs,
    step_raw,
    step_bias,
    decay_log,
    skip_gain,
    filter_inner,
    filter_state,
    norm_gain,
    prompt_lengths,
    request_prompt,
):
    shape = jax.ShapeDtypeStruct
    seq = lax.axis_size("seq")
    place = lax.axis_index("seq").astype(jnp.int32)
    column = lax.axis_index("head").astype(jnp.int32)
    heads = step_bias.shape[0]
    places = jnp.stack([place, column, (128 - heads * column) % 128])
    heads_in = jnp.concatenate(
        [
            jnp.pad(step_bias, (0, 128 - heads))[None],
            jnp.pad(decay_log, (0, 128 - heads))[None],
            jnp.repeat(skip_gain, HEAD).reshape(8, 128),
            jnp.zeros((6, 128), F32),
        ],
        axis=0,
    )
    taps = jnp.concatenate([filter_inner, filter_state], axis=1)
    packed = call(
        pack_kernel,
        (head_inputs, state_proj, step_raw),
        shape((8, 16, WIDE + 128), BF16),
    )
    rows = lax.all_to_all(packed, "head", 0, 0).reshape(ROWS, WIDE + 128)
    halo = lax.ppermute(
        rows[ROWS - 8 :, :WIDE], "seq", [(source, source + 1) for source in range(seq - 1)]
    )
    message, act, decay, step = call(
        front_kernel,
        (places, prompt_lengths, request_prompt, rows, halo, taps, heads_in),
        (
            shape((64, MESSAGE, 128), BF16),
            shape((ROWS, WIDE), BF16),
            shape((ROWS, 128), F32),
            shape((ROWS, 128), F32),
        ),
        (pltpu.VMEM((ROWS + 8, WIDE), F32),),
        scalars=3,
    )
    got = lax.all_to_all(message, "seq", 0, 0)
    gate = lax.all_to_all(gate_inputs, "head", split_axis=1, concat_axis=0, tiled=True)
    own, inflow = call(
        within_kernel,
        (places, prompt_lengths, act, decay, step, gate, heads_in),
        (shape((ROWS, WIDTH), F32), shape((ROWS, WIDTH), F32)),
        scalars=2,
    )
    extra = later_ends(place, prompt_lengths, rows, halo, act, decay, step)
    answer = call(
        scan_kernel,
        (places, prompt_lengths, got, extra),
        shape((64, MESSAGE, 128), BF16),
        (pltpu.VMEM((64, 24, 128), F32), pltpu.VMEM((PROMPTS, 24, 128), F32)),
        scalars=2,
    )
    back = lax.all_to_all(answer, "seq", 0, 0)
    hidden, final, edge_inner, edge_state = call(
        back_kernel,
        (act, own, inflow, back, norm_gain[None]),
        (
            shape((ROWS, WIDTH), BF16),
            shape((WIDTH, STATE), F32),
            shape((1, 3, WIDTH), BF16),
            shape((1, 3, 256), BF16),
        ),
        (pltpu.VMEM((ROWS, WIDTH), F32),),
    )
    return hidden, final.reshape(1, heads, HEAD, STATE), edge_inner, edge_state


def solution(mesh):
    return jax.shard_map(
        per_device,
        mesh=mesh,
        in_specs=(
            P(("seq", "head"), None),
            P(("seq", "head"), None),
            P(("seq", "head"), None),
            P(("seq", "head"), None),
            P("head"),
            P("head"),
            P("head"),
            P(None, "head"),
            P(None, "head"),
            P("head"),
            P(),
            P("seq", None),
        ),
        out_specs=(
            P("seq", "head"),
            P("seq", "head", None, None),
            P("seq", None, "head"),
            P("seq", None, "head"),
        ),
        check_vma=False,
    )
```

```python
import jax
import jax.numpy as jnp
from jax import lax
from jax.experimental import pallas as pl
from jax.experimental.pallas import tpu as pltpu
from jax.sharding import Mesh
from jax.sharding import PartitionSpec as P

STATE = 128
EPSILON = 1e-05
PROMPTS = 7
HEAD = 64
BLOCK = 128
ZS, XS, HS = 16, 4, 8
ROW = 512
BLOCKS = ROW // BLOCK
WIDTH = 256
WIDE = 512
GATE = WIDE + 128
SENT = GATE + WIDTH
SLOTS = 3
TAIL = 16 * (SLOTS + 1)
BIG = 1 << 30
F32 = jnp.float32
BF16 = jnp.bfloat16


def dot(a, b, dims, precision=None):
    return lax.dot_general(a, b, (dims, ((), ())), precision=precision, preferred_element_type=F32)


def bounds(length_ref):
    starts, ends = [], []
    total = jnp.int32(0)
    for p in range(PROMPTS):
        starts.append(total)
        total = total + length_ref[p]
        ends.append(total - 1)
    return starts, ends


def segment_at(position, starts):
    found = jnp.zeros_like(position) - 1
    for start in starts:
        found = found + (position >= start).astype(jnp.int32)
    return found


def iota(shape, axis):
    return lax.broadcasted_iota(jnp.int32, shape, axis)


def spread(weights, tile, lane):
    left = jnp.broadcast_to(weights[:, 2 * tile : 2 * tile + 1], lane.shape)
    right = jnp.broadcast_to(weights[:, 2 * tile + 1 : 2 * tile + 2], lane.shape)
    return jnp.where(lane < HEAD, left, right)


def laid_out(value, at, lane):
    value = jnp.where(lane < 4, value, 0.0)
    first = value.astype(BF16).astype(F32)
    second = (value - first).astype(BF16).astype(F32)
    third = value - first - second
    out = jnp.zeros_like(value)
    for k, part in enumerate((first, second, third)):
        shift = at + 4 * k
        out = out + (pltpu.roll(part, shift, 1) if shift else part)
    return out


def picks(head, at):
    lane = iota((128, 128), 0)
    return ((lane == at + head) | (lane == at + 4 + head) | (lane == at + 8 + head)).astype(BF16)


def pack_kernel(request_ref, inner_ref, proj_ref, step_ref, gate_ref, out_ref):
    step = step_ref[...].astype(F32)
    lane = iota(step.shape, 1)
    request = request_ref[0, 0].astype(F32)
    for q in range(XS):
        for h in range(HS):
            at = q * HS + h
            col = h * 1024 + q * WIDTH
            out_ref[at, :, 0:WIDTH] = inner_ref[:, col : col + WIDTH]
            out_ref[at, :, WIDTH:WIDE] = proj_ref[:, h * 256 : (h + 1) * 256]
            shift = (128 - (16 * h + 4 * q)) % 128
            own = pltpu.roll(step, shift, 1) if shift else step
            out_ref[at, :, WIDE:GATE] = jnp.where(lane == 4, request, own).astype(BF16)
            out_ref[at, :, GATE:] = gate_ref[:, col : col + WIDTH]


def front_kernel(
    place_ref, length_ref, rows_ref, halo_ref, inner_taps_ref, state_taps_ref, head_ref,
    message_ref, act_ref, decay_ref, step_ref, padded, weighted,
):
    first = place_ref[0] * ROW
    quarter = place_ref[1]
    starts, ends = bounds(length_ref)
    lane = iota((BLOCK, 128), 1)
    sub = iota((BLOCK, 128), 0)
    before = segment_at(first - 1, starts)
    last = segment_at(first + ROW - 1, starts)
    found = [[jnp.int32(BIG), jnp.int32(-2), jnp.int32(0)] for _ in range(SLOTS)]
    count = jnp.int32(0)
    for p in range(PROMPTS):
        here = (ends[p] >= first) & (ends[p] < first + ROW)
        for m in range(SLOTS):
            mine = here & (count == m)
            for at, value in enumerate((ends[p], jnp.int32(p), starts[p])):
                found[m][at] = jnp.where(mine, value, found[m][at])
        count = count + here.astype(jnp.int32)
    heads = pltpu.roll(head_ref[...], place_ref[2], 1)
    bias = heads[0:1, :]
    scale = -jnp.exp(heads[1:2, :])
    lower = (sub >= lane).astype(F32)

    padded[0:8, :] = halo_ref[...].astype(F32)
    padded[8:, :] = rows_ref[:, 0:WIDE].astype(F32)
    carry = jnp.zeros((1, 128), F32)
    for b in range(BLOCKS):
        rows = slice(b * BLOCK, (b + 1) * BLOCK)
        position = sub + (first + b * BLOCK)
        row_start = jnp.zeros_like(position)
        for start in starts:
            row_start = jnp.where(position >= start, start, row_start)
        inside = [(position - 3 + k) >= row_start for k in range(4)]
        for tile in range(WIDE // 128):
            cols = slice(tile * 128, (tile + 1) * 128)
            total = jnp.zeros((BLOCK, 128), F32)
            for k in range(4):
                if tile < 2:
                    at = pl.multiple_of(quarter * WIDTH + tile * 128, 128)
                    taps = inner_taps_ref[k : k + 1, pl.ds(at, 128)]
                else:
                    taps = state_taps_ref[k : k + 1, (tile - 2) * 128 : (tile - 1) * 128]
                at = b * BLOCK + 5 + k
                total = total + jnp.where(inside[k], padded[at : at + BLOCK, cols], 0.0) * taps
            act_ref[rows, cols] = (total * jax.nn.sigmoid(total)).astype(BF16)
        step = jax.nn.softplus(rows_ref[rows, WIDE:GATE].astype(F32) + bias)
        decay = dot(lower, step * scale, ((1,), (0,)), lax.Precision.HIGHEST) + carry
        carry = decay[BLOCK - 1 : BLOCK, :]
        step_ref[rows, :] = step
        decay_ref[rows, :] = decay
    row = iota((1, 128), 1)
    index = iota((8, 128), 0)
    small = laid_out(jnp.where(last == before, jnp.exp(carry), 0.0), 0, row)
    edges = []
    for m in range(-1, SLOTS):
        if m < 0:
            end_decay = carry
        else:
            end, prompt, start = found[m]
            some = end < BIG
            local = jnp.where(some, end - first, 0)
            end_decay = decay_ref[pl.ds(local, 1), :]
        for b in range(BLOCKS):
            rows = slice(b * BLOCK, (b + 1) * BLOCK)
            position = sub + (first + b * BLOCK)
            if m < 0:
                member = segment_at(position, starts) == last
            else:
                member = some & (position >= start) & (position <= end)
            gap = jnp.minimum(end_decay - decay_ref[rows, :], 0.0)
            weights = jnp.where(member, jnp.exp(gap), 0.0) * step_ref[rows, :]
            for tile in range(2):
                cols = slice(tile * 128, (tile + 1) * 128)
                weighted[rows, cols] = (spread(weights, tile, lane) * act_ref[rows, cols].astype(F32)).astype(BF16)
        at = 16 * (m + 1)
        for tile in range(2):
            state = dot(weighted[:, tile * 128 : (tile + 1) * 128], act_ref[:, WIDTH : WIDTH + STATE], ((0,), (0,)))
            message_ref[tile * 8 : (tile + 1) * 8, at : at + 16, :] = state.astype(BF16).reshape(8, 16, 128)
        if m < 0:
            continue
        carried = jnp.where(some & (prompt == before), jnp.exp(end_decay), 0.0)
        small = small + laid_out(carried, 12 * (m + 1), row)
        edge = []
        for k in range(3):
            valid = some & (end - 2 + k >= start)
            edge.append(jnp.where(valid, padded[pl.ds(8 + local - 2 + k, 1), :], 0.0))
        edges.append(edge)
    for k in range(XS):
        request = rows_ref[k * BLOCK : k * BLOCK + 8, WIDE:GATE].astype(F32)[0:1, :]
        small = small + jnp.where(row == 64 + k, pltpu.roll(request, 60 + k, 1), 0.0)
    block = jnp.where(index == SLOTS, small, jnp.zeros((8, 128), F32))
    for k in range(ZS):
        value = block
        if k < 12:
            for m in range(SLOTS):
                piece = edges[m][k // 4][:, (k % 4) * 128 : (k % 4 + 1) * 128]
                value = jnp.where(index == m, piece, value)
        message_ref[k, TAIL : TAIL + 8, :] = value.astype(BF16)


def scan_kernel(place_ref, length_ref, got_ref, extra_ref, out_ref, small, states, finals):
    _, ends = bounds(length_ref)
    head = place_ref[0] // 4
    one = [picks(head, 12 * m) for m in range(SLOTS + 1)]
    one = one + [(iota((128, 128), 0) == 64 + k).astype(BF16) for k in range(XS)]
    small[...] = dot(got_ref[:, TAIL : TAIL + 8, :].reshape(ZS * 8, 128), jnp.concatenate(one, axis=1), ((1,), (0,)))
    state = jnp.zeros((16, 128), F32)
    for j in range(ZS):
        states[j] = state
        out_ref[j, 0:16, :] = state.astype(BF16)
        at = 8 * j + SLOTS
        state = small[at : at + 1, 0:128] * state + got_ref[j, 0:16, :].astype(F32)
    for p in range(PROMPTS):
        z = ends[p] // ROW
        rank = jnp.int32(0)
        for other in range(p):
            rank = rank + (ends[other] // ROW == z).astype(jnp.int32)
        value = extra_ref[p]
        state = states[z]
        tail = got_ref[z, TAIL : TAIL + 8, :].astype(F32)
        factor = small[pl.ds(8 * z + SLOTS, 1), 128 : 128 * (SLOTS + 1)]
        for m in range(SLOTS):
            own = got_ref[z, 16 * m + 16 : 16 * m + 32, :].astype(F32) + factor[:, 128 * m : 128 * (m + 1)] * state
            edge = jnp.broadcast_to(tail[m : m + 1, :], (8, 128))
            value = jnp.where(rank == m, jnp.concatenate([own, edge], axis=0), value)
        finals[p] = value
    index = iota((8, 128), 0)
    for z in range(ZS):
        edges = jnp.zeros((8, 128), F32)
        for k in range(XS):
            at = 128 * (SLOTS + 1 + k)
            request = small[8 * z + SLOTS : 8 * z + SLOTS + 1, at : at + 128]
            value = finals[0]
            for p in range(1, PROMPTS):
                value = jnp.where(request == float(p), finals[p], value)
            out_ref[z, 16 * k + 16 : 16 * k + 32, :] = value[0:16].astype(BF16)
            edges = jnp.where(index == k, value[16:24], edges)
        out_ref[z, 80:88, :] = edges.astype(BF16)


def within_kernel(
    place_ref, length_ref, act_ref, decay_ref, step_ref, rows_ref, skip_ref, own_ref, in_ref, carried,
):
    first = place_ref[0] * ROW
    quarter = place_ref[1]
    starts, _ = bounds(length_ref)
    before_row = segment_at(first - 1, starts)
    lane = iota((BLOCK, 128), 1)
    sub = iota((BLOCK, 128), 0)
    carry = jnp.zeros((1, 128), F32)
    for b in range(BLOCKS):
        rows = slice(b * BLOCK, (b + 1) * BLOCK)
        at = first + b * BLOCK
        before = segment_at(at - 1, starts)
        last = segment_at(at + BLOCK - 1, starts)
        segment = segment_at(sub + at, starts)
        causal = (segment == segment_at(lane + at, starts)) & (sub >= lane)
        write = act_ref[rows, WIDTH : WIDTH + STATE]
        read = act_ref[rows, WIDTH + STATE : WIDE]
        scores = dot(read, write, ((1,), (1,)))
        decay = decay_ref[rows, :]
        step = step_ref[rows, :]
        decay_t = decay.T
        step_t = step.T
        inflow = jnp.where(segment == before, jnp.exp(jnp.minimum(decay - carry, 0.0)), 0.0)
        inflow_row = jnp.where(segment == before_row, jnp.exp(decay), 0.0)
        end = decay[BLOCK - 1 : BLOCK, :]
        tail = jnp.where(segment == last, jnp.exp(jnp.minimum(end - decay, 0.0)), 0.0) * step
        keep = jnp.where(last == before, jnp.exp(end - carry), 0.0)
        for tile in range(2):
            cols = slice(tile * 128, (tile + 1) * 128)
            x = act_ref[rows, cols]
            mixing = []
            for head in (2 * tile, 2 * tile + 1):
                gap = decay[:, head : head + 1] - decay_t[head : head + 1, :]
                weight = jnp.exp(jnp.where(causal, gap, -jnp.inf))
                mixing.append((scores * weight * step_t[head : head + 1, :]).astype(BF16))
            none = jnp.zeros_like(x)
            both = jnp.concatenate([jnp.where(lane < HEAD, x, none), jnp.where(lane < HEAD, none, x)], axis=0)
            value = dot(jnp.concatenate(mixing, axis=1), both, ((1,), (0,)))
            skip = skip_ref[0:1, pl.ds(pl.multiple_of(quarter * WIDTH + tile * 128, 128), 128)]
            value = value + skip * x.astype(F32)
            if b:
                across = dot(read.astype(F32), carried[tile], ((1,), (1,)), lax.Precision.HIGHEST)
                value = value + spread(inflow, tile, lane) * across
            gate = rows_ref[rows, GATE + tile * 128 : GATE + (tile + 1) * 128].astype(F32)
            gate = gate * jax.nn.sigmoid(gate)
            own_ref[rows, cols] = value * gate
            in_ref[rows, cols] = spread(inflow_row, tile, lane) * gate
            if b < BLOCKS - 1:
                weighted = (spread(tail, tile, lane) * x.astype(F32)).astype(BF16)
                state = dot(weighted, write, ((0,), (0,)))
                if b:
                    factor = jnp.where(sub < HEAD, keep[:, 2 * tile : 2 * tile + 1], keep[:, 2 * tile + 1 : 2 * tile + 2])
                    state = factor * carried[tile] + state
                carried[tile] = state
        carry = end


def across_kernel(act_ref, own_ref, in_ref, got_ref, out_ref):
    for tile in range(2):
        cols = slice(tile * 128, (tile + 1) * 128)
        state = got_ref[tile * 8 : (tile + 1) * 8, 0:16, :].reshape(128, 128)
        for b in range(BLOCKS):
            rows = slice(b * BLOCK, (b + 1) * BLOCK)
            across = dot(act_ref[rows, WIDTH + STATE : WIDE], state, ((1,), (1,)))
            value = own_ref[rows, cols] + in_ref[rows, cols] * across
            out_ref[b, tile * BLOCK : (tile + 1) * BLOCK, :] = value.astype(BF16)
    index = iota((16, 128), 0)
    edges = [jnp.zeros((16, 128), F32) for _ in range(XS)]
    for i in range(ZS):
        tail = got_ref[i, 80:88, :].astype(F32)
        for k in range(XS):
            at = 2 * BLOCK + 16 * i
            out_ref[k, at : at + 16, :] = got_ref[i, 16 * k + 16 : 16 * k + 32, :]
            if i < 12:
                edges[k] = jnp.where(index == i, tail[k : k + 1, :], edges[k])
    for k in range(XS):
        out_ref[k, 512:528, :] = edges[k].astype(BF16)


def last_kernel(got_ref, gain_ref, hidden_ref, final_ref, inner_ref, proj_ref):
    total = jnp.zeros((BLOCK, 128), F32)
    for q in range(XS):
        for tile in range(2):
            value = got_ref[q, tile * BLOCK : (tile + 1) * BLOCK, :].astype(F32)
            total = total + value * value
    mean = jnp.sum(total, axis=1, keepdims=True) * (1.0 / (XS * WIDTH))
    inverse = lax.rsqrt(mean + EPSILON)
    for q in range(XS):
        for tile in range(2):
            cols = slice(q * WIDTH + tile * 128, q * WIDTH + (tile + 1) * 128)
            value = got_ref[q, tile * BLOCK : (tile + 1) * BLOCK, :].astype(F32)
            hidden_ref[:, cols] = ((value * inverse) * gain_ref[:, cols]).astype(BF16)
        final_ref[q * WIDTH : (q + 1) * WIDTH, :] = got_ref[q, 256:512, :].astype(F32)
        edges = got_ref[q, 512:528, :].astype(F32)
        for k in range(3):
            for c in range(2):
                at = q * WIDTH + c * 128
                inner_ref[0, k : k + 1, at : at + 128] = edges[4 * k + c : 4 * k + c + 1, :].astype(BF16)
                if q == 0:
                    proj_ref[0, k : k + 1, c * 128 : (c + 1) * 128] = edges[4 * k + 2 + c : 4 * k + 3 + c, :].astype(BF16)


def call(kernel, ins, outs, scratch=(), scalars=0, limit=24 << 20):
    smem = pl.BlockSpec(memory_space=pltpu.SMEM)
    vmem = pl.BlockSpec(memory_space=pltpu.VMEM)
    return pl.pallas_call(
        kernel,
        out_shape=outs,
        in_specs=[smem] * scalars + [vmem] * (len(ins) - scalars),
        out_specs=jax.tree.map(lambda _: vmem, outs),
        scratch_shapes=list(scratch),
        compiler_params=pltpu.CompilerParams(vmem_limit_bytes=limit),
    )(*ins)


def exchange(sent, place):
    k = jnp.arange(ZS, dtype=jnp.int32)
    held = sent[(k + place) % ZS]
    for shift in (1, 2, 4, 8):
        moved = lax.ppermute(held, "z", [(source, (source + shift) % ZS) for source in range(ZS)])
        held = jnp.where(((k & shift) != 0)[:, None, None], moved, held)
    return held[(place - k) % ZS]


def later_ends(place, prompt_lengths, rows, halo, act, decay, step):
    ends = jnp.cumsum(prompt_lengths) - 1
    starts = ends + 1 - prompt_lengths
    ids = jnp.arange(PROMPTS, dtype=jnp.int32)
    z = ends // ROW
    rank = jnp.sum((z[None, :] == z[:, None]) & (ids[None, :] < ids[:, None]), axis=1)
    position = place * ROW + jnp.arange(ROW, dtype=jnp.int32)

    def step_of(carry):
        k, extra = carry
        mine = (z == place) & (rank == k)
        some = jnp.any(mine)
        end = jnp.sum(jnp.where(mine, ends, 0))
        start = jnp.sum(jnp.where(mine, starts, 0))
        member = some & (position >= start) & (position <= end)
        end_decay = jnp.sum(jnp.where((position == end)[:, None], decay, 0.0), axis=0, keepdims=True)
        weights = jnp.where(member[:, None], jnp.exp(jnp.minimum(end_decay - decay, 0.0)), 0.0) * step
        weights = weights[:, : WIDTH // HEAD]
        x = act[:, :WIDTH].reshape(ROW, -1, HEAD).astype(F32)
        weighted = (weights[:, :, None] * x).reshape(ROW, WIDTH).astype(BF16)
        own = dot(weighted, act[:, WIDTH : WIDTH + STATE], ((0,), (0,))).astype(BF16)
        padded = jnp.concatenate([halo, rows[:, :WIDE]], axis=0)
        wanted = end - 2 + jnp.arange(3, dtype=jnp.int32)
        onehot = (jnp.arange(ROW + 8)[None, :] + (place * ROW - 8) == wanted[:, None]) & some
        onehot = onehot & (wanted >= start)[:, None]
        edge = dot(onehot.astype(BF16), padded, ((1,), (0,))).astype(BF16)
        edge = jnp.pad(edge.reshape(12, 1, 128), ((0, 4), (0, 7), (0, 0)))
        sent = jnp.concatenate([own.reshape(ZS, 16, 128), edge], axis=1)
        taken = exchange(sent, place)[z].astype(F32)
        taken = jnp.concatenate([taken[:, :16], jnp.broadcast_to(taken[:, 16:17], (PROMPTS, 8, 128))], axis=1)
        return k + 1, jnp.where((rank == k)[:, None, None], taken, extra)

    most = jnp.max(rank)
    none = jnp.zeros((PROMPTS, 24, 128), F32)
    return lax.cond(
        most >= SLOTS,
        lambda: lax.while_loop(lambda carry: carry[0] <= most, step_of, (jnp.full_like(most, SLOTS), none))[1],
        lambda: none,
    )


def per_device(
    head_inputs,
    state_proj,
    gate_inputs,
    step_raw,
    step_bias,
    decay_log,
    skip_gain,
    filter_inner,
    filter_state,
    norm_gain,
    prompt_lengths,
    request_prompt,
):
    shape = jax.ShapeDtypeStruct
    place = lax.axis_index("z").astype(jnp.int32)
    quarter = lax.axis_index("x").astype(jnp.int32)
    heads = step_bias.shape[0]
    places = jnp.stack([place, quarter, (128 - 4 * quarter) % 128])
    heads_in = jnp.pad(jnp.stack([step_bias, decay_log]), ((0, 6), (0, 128 - heads)))
    skip = jnp.repeat(skip_gain, HEAD)[None]
    packed = call(
        pack_kernel,
        (request_prompt, head_inputs, state_proj, step_raw, gate_inputs),
        shape((XS * HS, 16, SENT), BF16),
        scalars=1,
        limit=None,
    )
    rows = lax.all_to_all(packed, ("x", "head"), 0, 0).reshape(ROW, SENT)
    halo = lax.ppermute(rows[ROW - 8 :, :WIDE], "z", [(source, source + 1) for source in range(ZS - 1)])
    message, act, decay, step = call(
        front_kernel,
        (places, prompt_lengths, rows, halo, filter_inner, filter_state, heads_in),
        (
            shape((ZS, TAIL + 8, 128), BF16),
            shape((ROW, WIDE), BF16),
            shape((ROW, 128), F32),
            shape((ROW, 128), F32),
        ),
        (pltpu.VMEM((ROW + 8, WIDE), F32), pltpu.VMEM((ROW, WIDTH), BF16)),
        scalars=2,
    )
    got = lax.all_to_all(message, "z", 0, 0)
    own, inflow = call(
        within_kernel,
        (places, prompt_lengths, act, decay, step, rows, skip),
        (shape((ROW, WIDTH), F32), shape((ROW, WIDTH), F32)),
        (pltpu.VMEM((2, 128, 128), F32),),
        scalars=2,
    )
    own, rows, halo, act, decay, step = lax.optimization_barrier((own, rows, halo, act, decay, step))
    extra = later_ends(place, prompt_lengths, rows, halo, act, decay, step)
    answer = call(
        scan_kernel,
        (places, prompt_lengths, got, extra),
        shape((ZS, 88, 128), BF16),
        (
            pltpu.VMEM((ZS * 8, 128 * (SLOTS + 1 + XS)), F32),
            pltpu.VMEM((ZS, 16, 128), F32),
            pltpu.VMEM((PROMPTS, 24, 128), F32),
        ),
        scalars=2,
    )
    back = lax.all_to_all(answer, "z", 0, 0)
    shared = call(across_kernel, (act, own, inflow, back), shape((XS, 528, 128), BF16))
    shared = lax.all_to_all(shared, "x", 0, 0)
    hidden, final, edge_inner, edge_state = call(
        last_kernel,
        (shared, norm_gain[None]),
        (
            shape((BLOCK, XS * WIDTH), BF16),
            shape((XS * WIDTH, STATE), F32),
            shape((1, 3, XS * WIDTH), BF16),
            shape((1, 3, 256), BF16),
        ),
    )
    return hidden, final.reshape(1, heads, HEAD, STATE), edge_inner, edge_state


def solution(mesh):
    seq = ("z", "x")
    mesh = Mesh(mesh.devices.reshape(ZS, XS, HS), ("z", "x", "head"))
    tokens = P(("z", "x", "head"), None)
    return jax.shard_map(
        per_device,
        mesh=mesh,
        in_specs=(
            tokens,
            tokens,
            tokens,
            tokens,
            P("head"),
            P("head"),
            P("head"),
            P(None, "head"),
            P(None, "head"),
            P("head"),
            P(),
            P(seq, None),
        ),
        out_specs=(
            P(seq, "head"),
            P(seq, "head", None, None),
            P(seq, None, "head"),
            P(seq, None, "head"),
        ),
        check_vma=False,
    )
```

```python
import functools

import jax
import jax.numpy as jnp
from jax import lax
from jax.experimental import pallas as pl
from jax.experimental.pallas import tpu as pltpu
from jax.sharding import Mesh
from jax.sharding import PartitionSpec as P

STATE = 128
EPSILON = 1e-05
PROMPTS = 7
HEAD = 64
BLOCK = 128
ZS, XS, HS = 16, 4, 8
ROW = 512
BLOCKS = ROW // BLOCK
WIDTH = 256
WIDE = 512
STEPS, GATE, SENT = 64, 72, 104
FEW = 2
REQUEST = 96
BIG = 1 << 30
F32 = jnp.float32
BF16 = jnp.bfloat16


def dot(a, b, dims, precision=None):
    return lax.dot_general(a, b, (dims, ((), ())), precision=precision, preferred_element_type=F32)


def bounds(length_ref):
    starts, ends = [], []
    total = jnp.int32(0)
    for p in range(PROMPTS):
        starts.append(total)
        total = total + length_ref[p]
        ends.append(total - 1)
    return starts, ends


def segment_at(position, starts):
    found = jnp.zeros_like(position) - 1
    for start in starts:
        found = found + (position >= start).astype(jnp.int32)
    return found


def iota(shape, axis):
    return lax.broadcasted_iota(jnp.int32, shape, axis)


def spread(weights, tile, lane):
    left = jnp.broadcast_to(weights[:, 2 * tile : 2 * tile + 1], lane.shape)
    right = jnp.broadcast_to(weights[:, 2 * tile + 1 : 2 * tile + 2], lane.shape)
    return jnp.where(lane < HEAD, left, right)


def laid_out(value, at, lane):
    value = jnp.where(lane < 4, value, 0.0)
    first = value.astype(BF16).astype(F32)
    second = (value - first).astype(BF16).astype(F32)
    third = value - first - second
    out = jnp.zeros_like(value)
    for k, part in enumerate((first, second, third)):
        shift = at + 4 * k
        out = out + (pltpu.roll(part, shift, 1) if shift else part)
    return out


def picks(head, at):
    lane = iota((128, 128), 0)
    return ((lane == at + head) | (lane == at + 4 + head) | (lane == at + 8 + head)).astype(BF16)


def pack_kernel(request_ref, inner_ref, proj_ref, step_ref, gate_ref, out_ref):
    step = step_ref[...].astype(F32)
    lane = iota((8, 128), 1)
    request = request_ref[0, 0].astype(F32)
    for q in range(XS):
        for h in range(HS):
            at = q * HS + h
            for c in range(2):
                col = h * 1024 + q * WIDTH + c * 128
                out_ref[at, c * 16 : c * 16 + 16, :] = inner_ref[:, col : col + 128]
                out_ref[at, GATE + c * 16 : GATE + c * 16 + 16, :] = gate_ref[:, col : col + 128]
                col = h * 256 + c * 128
                out_ref[at, 32 + c * 16 : 48 + c * 16, :] = proj_ref[:, col : col + 128]
            shift = (128 - (16 * h + 4 * q)) % 128
            early = pltpu.roll(step[0:8], shift, 1) if shift else step[0:8]
            shift = (shift + 64) % 128
            late = pltpu.roll(step[8:16], shift, 1) if shift else step[8:16]
            own = jnp.where(lane < 64, early, late)
            out_ref[at, STEPS:GATE, :] = jnp.where(lane == 4, request, own).astype(BF16)


def block_of(rows_ref, b, row):
    return rows_ref[8 * b : 8 * b + 8, row : row + 16, :].reshape(BLOCK, 128)


def steps_of(rows_ref, b):
    early = rows_ref[8 * b : 8 * b + 8, STEPS:GATE, :].astype(F32)
    late = pltpu.roll(early.reshape(64, 128), 64, 1).reshape(8, 8, 128)
    return jnp.concatenate([early, late], axis=1).reshape(BLOCK, 128)


def padded_rows(rows_ref, halo_ref, padded):
    for tile in range(WIDE // 128):
        cols = slice(tile * 128, (tile + 1) * 128)
        padded[0:8, cols] = halo_ref[tile].astype(F32)
        for b in range(BLOCKS):
            at = 8 + b * BLOCK
            padded[at : at + BLOCK, cols] = block_of(rows_ref, b, tile * 16).astype(F32)


def weigh(weighted, act_ref, decay_ref, step_ref, end_decay, member_of):
    lane = iota((BLOCK, 128), 1)
    for b in range(BLOCKS):
        rows = slice(b * BLOCK, (b + 1) * BLOCK)
        gap = jnp.minimum(end_decay - decay_ref[rows, :], 0.0)
        weights = jnp.where(member_of(b), jnp.exp(gap), 0.0) * step_ref[rows, :]
        for tile in range(2):
            cols = slice(tile * 128, (tile + 1) * 128)
            weighted[rows, cols] = (spread(weights, tile, lane) * act_ref[rows, cols].astype(F32)).astype(BF16)


def send_state(message_ref, at, weighted, act_ref):
    for tile in range(2):
        state = dot(weighted[:, tile * 128 : (tile + 1) * 128], act_ref[:, WIDTH : WIDTH + STATE], ((0,), (0,)))
        message_ref[tile * 8 : (tile + 1) * 8, at : at + 16, :] = state.astype(BF16).reshape(8, 16, 128)


def send_ends(slots, first, length_ref, rows_ref, act_ref, decay_ref, step_ref, message_ref, padded, weighted):
    starts, ends = bounds(length_ref)
    before = segment_at(first - 1, starts)
    last = segment_at(first + ROW - 1, starts)
    sub = iota((BLOCK, 128), 0)
    row = iota((1, 128), 1)
    index = iota((8, 128), 0)
    found = [[jnp.int32(BIG), jnp.int32(-2), jnp.int32(0)] for _ in range(slots)]
    count = jnp.int32(0)
    for p in range(PROMPTS):
        here = (ends[p] >= first) & (ends[p] < first + ROW)
        for m in range(slots):
            mine = here & (count == m)
            for at, value in enumerate((ends[p], jnp.int32(p), starts[p])):
                found[m][at] = jnp.where(mine, value, found[m][at])
        count = count + here.astype(jnp.int32)
    carry = decay_ref[ROW - 1 : ROW, :]
    small = laid_out(jnp.where(last == before, jnp.exp(carry), 0.0), 0, row)
    edges = []
    for m in range(slots):
        end, prompt, start = found[m]
        some = end < BIG
        local = jnp.where(some, end - first, 0)
        end_decay = decay_ref[pl.ds(local, 1), :]
        at = 16 * (m + 1)

        @pl.when(some)
        def _(end=end, start=start, end_decay=end_decay, at=at):
            def member_of(b):
                position = sub + (first + b * BLOCK)
                return (position >= start) & (position <= end)

            weigh(weighted, act_ref, decay_ref, step_ref, end_decay, member_of)
            send_state(message_ref, at, weighted, act_ref)

        @pl.when(jnp.logical_not(some))
        def _(at=at):
            message_ref[:, at : at + 16, :] = jnp.zeros((ZS, 16, 128), BF16)

        carried = jnp.where(some & (prompt == before), jnp.exp(end_decay), 0.0)
        small = small + laid_out(carried, 12 * (m + 1), row)
        edge = []
        for k in range(3):
            valid = some & (end - 2 + k >= start)
            edge.append(jnp.where(valid, padded[pl.ds(8 + local - 2 + k, 1), :], 0.0))
        edges.append(edge)
    for k in range(XS):
        request = rows_ref[k * 8, STEPS:GATE, :].astype(F32)[0:1, :]
        small = small + jnp.where(row == REQUEST + k, pltpu.roll(request, REQUEST - 4 + k, 1), 0.0)
    block = jnp.where(index == slots, small, jnp.zeros((8, 128), F32))
    tail = 16 * (slots + 1)
    for k in range(ZS):
        value = block
        if k < 12:
            for m in range(slots):
                piece = edges[m][k // 4][:, (k % 4) * 128 : (k % 4 + 1) * 128]
                value = jnp.where(index == m, piece, value)
        message_ref[k, tail : tail + 8, :] = value.astype(BF16)


def front_kernel(
    place_ref, length_ref, rows_ref, halo_ref, inner_taps_ref, state_taps_ref, head_ref,
    message_ref, act_ref, decay_ref, step_ref, padded, weighted,
):
    first = place_ref[0] * ROW
    quarter = place_ref[1]
    starts, _ = bounds(length_ref)
    sub = iota((BLOCK, 128), 0)
    last = segment_at(first + ROW - 1, starts)
    heads = pltpu.roll(head_ref[...], place_ref[2], 1)
    bias = heads[0:1, :]
    scale = -jnp.exp(heads[1:2, :])
    lower = (sub >= iota((BLOCK, 128), 1)).astype(F32)

    padded_rows(rows_ref, halo_ref, padded)
    carry = jnp.zeros((1, 128), F32)
    for b in range(BLOCKS):
        rows = slice(b * BLOCK, (b + 1) * BLOCK)
        position = sub + (first + b * BLOCK)
        row_start = jnp.zeros_like(position)
        for start in starts:
            row_start = jnp.where(position >= start, start, row_start)
        inside = [(position - 3 + k) >= row_start for k in range(4)]
        for tile in range(WIDE // 128):
            cols = slice(tile * 128, (tile + 1) * 128)
            total = jnp.zeros((BLOCK, 128), F32)
            for k in range(4):
                if tile < 2:
                    at = pl.multiple_of(quarter * WIDTH + tile * 128, 128)
                    taps = inner_taps_ref[k : k + 1, pl.ds(at, 128)]
                else:
                    taps = state_taps_ref[k : k + 1, (tile - 2) * 128 : (tile - 1) * 128]
                at = b * BLOCK + 5 + k
                total = total + jnp.where(inside[k], padded[at : at + BLOCK, cols], 0.0) * taps
            act_ref[rows, cols] = (total * jax.nn.sigmoid(total)).astype(BF16)
        step = jax.nn.softplus(steps_of(rows_ref, b) + bias)
        decay = dot(lower, step * scale, ((1,), (0,)), lax.Precision.HIGHEST) + carry
        carry = decay[BLOCK - 1 : BLOCK, :]
        step_ref[rows, :] = step
        decay_ref[rows, :] = decay

    def member_of(b):
        return segment_at(sub + (first + b * BLOCK), starts) == last

    weigh(weighted, act_ref, decay_ref, step_ref, carry, member_of)
    send_state(message_ref, 0, weighted, act_ref)
    send_ends(FEW, first, length_ref, rows_ref, act_ref, decay_ref, step_ref, message_ref, padded, weighted)


def many_kernel(
    place_ref, length_ref, rows_ref, halo_ref, act_ref, decay_ref, step_ref, few_ref, message_ref, padded, weighted,
):
    padded_rows(rows_ref, halo_ref, padded)
    message_ref[:, 0:16, :] = few_ref[:, 0:16, :]
    send_ends(
        PROMPTS, place_ref[0] * ROW, length_ref, rows_ref, act_ref, decay_ref, step_ref, message_ref, padded, weighted
    )


def scan_kernel(slots, place_ref, length_ref, got_ref, out_ref, small, states, finals):
    _, ends = bounds(length_ref)
    head = place_ref[0] // 4
    tail_at = 16 * (slots + 1)
    one = [picks(head, 12 * m) for m in range(slots + 1)]
    one = one + [(iota((128, 128), 0) == REQUEST + k).astype(BF16) for k in range(XS)]
    small[...] = dot(got_ref[:, tail_at : tail_at + 8, :].reshape(ZS * 8, 128), jnp.concatenate(one, axis=1), ((1,), (0,)))
    state = jnp.zeros((16, 128), F32)
    for j in range(ZS):
        states[j] = state
        out_ref[j, 0:16, :] = state.astype(BF16)
        at = 8 * j + slots
        state = small[at : at + 1, 0:128] * state + got_ref[j, 0:16, :].astype(F32)
    for p in range(PROMPTS):
        z = ends[p] // ROW
        rank = jnp.int32(0)
        for other in range(p):
            rank = rank + (ends[other] // ROW == z).astype(jnp.int32)
        value = jnp.zeros((24, 128), F32)
        state = states[z]
        tail = got_ref[z, tail_at : tail_at + 8, :].astype(F32)
        factor = small[pl.ds(8 * z + slots, 1), 128 : 128 * (slots + 1)]
        for m in range(slots):
            own = got_ref[z, 16 * m + 16 : 16 * m + 32, :].astype(F32) + factor[:, 128 * m : 128 * (m + 1)] * state
            edge = jnp.broadcast_to(tail[m : m + 1, :], (8, 128))
            value = jnp.where(rank == m, jnp.concatenate([own, edge], axis=0), value)
        finals[p] = value
    index = iota((8, 128), 0)
    for z in range(ZS):
        edges = jnp.zeros((8, 128), F32)
        for k in range(XS):
            at = 128 * (slots + 1 + k)
            request = small[8 * z + slots : 8 * z + slots + 1, at : at + 128]
            value = finals[0]
            for p in range(1, PROMPTS):
                value = jnp.where(request == float(p), finals[p], value)
            out_ref[z, 16 * k + 16 : 16 * k + 32, :] = value[0:16].astype(BF16)
            edges = jnp.where(index == k, value[16:24], edges)
        out_ref[z, 80:88, :] = edges.astype(BF16)


def within_kernel(
    place_ref, length_ref, act_ref, decay_ref, step_ref, rows_ref, skip_ref, own_ref, in_ref, carried,
):
    first = place_ref[0] * ROW
    quarter = place_ref[1]
    starts, _ = bounds(length_ref)
    before_row = segment_at(first - 1, starts)
    lane = iota((BLOCK, 128), 1)
    sub = iota((BLOCK, 128), 0)
    carry = jnp.zeros((1, 128), F32)
    for b in range(BLOCKS):
        rows = slice(b * BLOCK, (b + 1) * BLOCK)
        at = first + b * BLOCK
        before = segment_at(at - 1, starts)
        last = segment_at(at + BLOCK - 1, starts)
        segment = segment_at(sub + at, starts)
        causal = (segment == segment_at(lane + at, starts)) & (sub >= lane)
        write = act_ref[rows, WIDTH : WIDTH + STATE]
        read = act_ref[rows, WIDTH + STATE : WIDE]
        scores = dot(read, write, ((1,), (1,)))
        decay = decay_ref[rows, :]
        step = step_ref[rows, :]
        decay_t = decay.T
        step_t = step.T
        inflow = jnp.where(segment == before, jnp.exp(jnp.minimum(decay - carry, 0.0)), 0.0)
        inflow_row = jnp.where(segment == before_row, jnp.exp(decay), 0.0)
        end = decay[BLOCK - 1 : BLOCK, :]
        tail = jnp.where(segment == last, jnp.exp(jnp.minimum(end - decay, 0.0)), 0.0) * step
        keep = jnp.where(last == before, jnp.exp(end - carry), 0.0)
        for tile in range(2):
            cols = slice(tile * 128, (tile + 1) * 128)
            x = act_ref[rows, cols]
            mixing = []
            for head in (2 * tile, 2 * tile + 1):
                gap = decay[:, head : head + 1] - decay_t[head : head + 1, :]
                weight = jnp.exp(jnp.where(causal, gap, -jnp.inf))
                mixing.append((scores * weight * step_t[head : head + 1, :]).astype(BF16))
            none = jnp.zeros_like(x)
            both = jnp.concatenate([jnp.where(lane < HEAD, x, none), jnp.where(lane < HEAD, none, x)], axis=0)
            value = dot(jnp.concatenate(mixing, axis=1), both, ((1,), (0,)))
            skip = skip_ref[0:1, pl.ds(pl.multiple_of(quarter * WIDTH + tile * 128, 128), 128)]
            value = value + skip * x.astype(F32)
            if b:
                across = dot(read.astype(F32), carried[tile], ((1,), (1,)), lax.Precision.HIGHEST)
                value = value + spread(inflow, tile, lane) * across
            gate = block_of(rows_ref, b, GATE + tile * 16).astype(F32)
            gate = gate * jax.nn.sigmoid(gate)
            own_ref[rows, cols] = value * gate
            in_ref[rows, cols] = spread(inflow_row, tile, lane) * gate
            if b < BLOCKS - 1:
                weighted = (spread(tail, tile, lane) * x.astype(F32)).astype(BF16)
                state = dot(weighted, write, ((0,), (0,)))
                if b:
                    factor = jnp.where(sub < HEAD, keep[:, 2 * tile : 2 * tile + 1], keep[:, 2 * tile + 1 : 2 * tile + 2])
                    state = factor * carried[tile] + state
                carried[tile] = state
        carry = end


def across_kernel(act_ref, own_ref, in_ref, got_ref, out_ref):
    for tile in range(2):
        cols = slice(tile * 128, (tile + 1) * 128)
        state = got_ref[tile * 8 : (tile + 1) * 8, 0:16, :].reshape(128, 128)
        for b in range(BLOCKS):
            rows = slice(b * BLOCK, (b + 1) * BLOCK)
            across = dot(act_ref[rows, WIDTH + STATE : WIDE], state, ((1,), (1,)))
            value = own_ref[rows, cols] + in_ref[rows, cols] * across
            out_ref[b, tile * BLOCK : (tile + 1) * BLOCK, :] = value.astype(BF16)
    index = iota((16, 128), 0)
    edges = [jnp.zeros((16, 128), F32) for _ in range(XS)]
    for i in range(ZS):
        tail = got_ref[i, 80:88, :].astype(F32)
        for k in range(XS):
            at = 2 * BLOCK + 16 * i
            out_ref[k, at : at + 16, :] = got_ref[i, 16 * k + 16 : 16 * k + 32, :]
            if i < 12:
                edges[k] = jnp.where(index == i, tail[k : k + 1, :], edges[k])
    for k in range(XS):
        out_ref[k, 512:528, :] = edges[k].astype(BF16)


def last_kernel(got_ref, gain_ref, hidden_ref, final_ref, inner_ref, proj_ref):
    total = jnp.zeros((BLOCK, 128), F32)
    for q in range(XS):
        for tile in range(2):
            value = got_ref[q, tile * BLOCK : (tile + 1) * BLOCK, :].astype(F32)
            total = total + value * value
    mean = jnp.sum(total, axis=1, keepdims=True) * (1.0 / (XS * WIDTH))
    inverse = lax.rsqrt(mean + EPSILON)
    for q in range(XS):
        for tile in range(2):
            cols = slice(q * WIDTH + tile * 128, q * WIDTH + (tile + 1) * 128)
            value = got_ref[q, tile * BLOCK : (tile + 1) * BLOCK, :].astype(F32)
            hidden_ref[:, cols] = ((value * inverse) * gain_ref[:, cols]).astype(BF16)
        final_ref[q * WIDTH : (q + 1) * WIDTH, :] = got_ref[q, 256:512, :].astype(F32)
        edges = got_ref[q, 512:528, :].astype(F32)
        for k in range(3):
            for c in range(2):
                at = q * WIDTH + c * 128
                inner_ref[0, k : k + 1, at : at + 128] = edges[4 * k + c : 4 * k + c + 1, :].astype(BF16)
                if q == 0:
                    proj_ref[0, k : k + 1, c * 128 : (c + 1) * 128] = edges[4 * k + 2 + c : 4 * k + 3 + c, :].astype(BF16)


def call(kernel, ins, outs, scratch=(), scalars=0, limit=24 << 20):
    smem = pl.BlockSpec(memory_space=pltpu.SMEM)
    vmem = pl.BlockSpec(memory_space=pltpu.VMEM)
    return pl.pallas_call(
        kernel,
        out_shape=outs,
        in_specs=[smem] * scalars + [vmem] * (len(ins) - scalars),
        out_specs=jax.tree.map(lambda _: vmem, outs),
        scratch_shapes=list(scratch),
        compiler_params=pltpu.CompilerParams(vmem_limit_bytes=limit),
    )(*ins)


def per_device(
    head_inputs,
    state_proj,
    gate_inputs,
    step_raw,
    step_bias,
    decay_log,
    skip_gain,
    filter_inner,
    filter_state,
    norm_gain,
    prompt_lengths,
    request_prompt,
):
    shape = jax.ShapeDtypeStruct
    place = lax.axis_index("z").astype(jnp.int32)
    quarter = lax.axis_index("x").astype(jnp.int32)
    heads = step_bias.shape[0]
    places = jnp.stack([place, quarter, (128 - 4 * quarter) % 128])
    heads_in = jnp.pad(jnp.stack([step_bias, decay_log]), ((0, 6), (0, 128 - heads)))
    skip = jnp.repeat(skip_gain, HEAD)[None]
    packed = call(
        pack_kernel,
        (request_prompt, head_inputs, state_proj, step_raw, gate_inputs),
        shape((XS * HS, SENT, 128), BF16),
        scalars=1,
        limit=None,
    )
    rows = lax.all_to_all(packed, ("x", "head"), 0, 0)
    halo = lax.ppermute(rows[-1, :STEPS].reshape(WIDE // 128, 16, 128)[:, 8:], "z", [(source, source + 1) for source in range(ZS - 1)])
    message, act, decay, step = call(
        front_kernel,
        (places, prompt_lengths, rows, halo, filter_inner, filter_state, heads_in),
        (
            shape((ZS, 16 * (FEW + 1) + 8, 128), BF16),
            shape((ROW, WIDE), BF16),
            shape((ROW, 128), F32),
            shape((ROW, 128), F32),
        ),
        (pltpu.VMEM((ROW + 8, WIDE), F32), pltpu.VMEM((ROW, WIDTH), BF16)),
        scalars=2,
    )
    scratch = (pltpu.VMEM((ROW + 8, WIDE), F32), pltpu.VMEM((ROW, WIDTH), BF16))

    def onward(slots, message):
        got = lax.all_to_all(message, "z", 0, 0)
        own, inflow = call(
            within_kernel,
            (places, prompt_lengths, act, decay, step, rows, skip),
            (shape((ROW, WIDTH), F32), shape((ROW, WIDTH), F32)),
            (pltpu.VMEM((2, 128, 128), F32),),
            scalars=2,
        )
        answer = call(
            functools.partial(scan_kernel, slots),
            (places, prompt_lengths, got),
            shape((ZS, 88, 128), BF16),
            (
                pltpu.VMEM((ZS * 8, 128 * (slots + 1 + XS)), F32),
                pltpu.VMEM((ZS, 16, 128), F32),
                pltpu.VMEM((PROMPTS, 24, 128), F32),
            ),
            scalars=2,
        )
        return answer, own, inflow

    def many():
        full = call(
            many_kernel,
            (places, prompt_lengths, rows, halo, act, decay, step, message),
            shape((ZS, 16 * (PROMPTS + 1) + 8, 128), BF16),
            scratch,
            scalars=2,
        )
        return onward(PROMPTS, full)

    z = (jnp.cumsum(prompt_lengths) - 1) // ROW
    most = jnp.max(jnp.sum((z[None, :] == z[:, None]).astype(jnp.int32), axis=1))
    answer, own, inflow = lax.cond(most > FEW, many, lambda: onward(FEW, message))
    back = lax.all_to_all(answer, "z", 0, 0)
    shared = call(across_kernel, (act, own, inflow, back), shape((XS, 528, 128), BF16))
    shared = lax.all_to_all(shared, "x", 0, 0)
    hidden, final, edge_inner, edge_state = call(
        last_kernel,
        (shared, norm_gain[None]),
        (
            shape((BLOCK, XS * WIDTH), BF16),
            shape((XS * WIDTH, STATE), F32),
            shape((1, 3, XS * WIDTH), BF16),
            shape((1, 3, 256), BF16),
        ),
    )
    return hidden, final.reshape(1, heads, HEAD, STATE), edge_inner, edge_state


def solution(mesh):
    seq = ("z", "x")
    mesh = Mesh(mesh.devices.reshape(ZS, XS, HS), ("z", "x", "head"))
    tokens = P(("z", "x", "head"), None)
    return jax.shard_map(
        per_device,
        mesh=mesh,
        in_specs=(
            tokens,
            tokens,
            tokens,
            tokens,
            P("head"),
            P("head"),
            P("head"),
            P(None, "head"),
            P(None, "head"),
            P("head"),
            P(),
            P(seq, None),
        ),
        out_specs=(
            P(seq, "head"),
            P(seq, "head", None, None),
            P(seq, None, "head"),
            P(seq, None, "head"),
        ),
        check_vma=False,
    )
```

```python
import functools

import jax
import jax.numpy as jnp
from jax import lax
from jax.experimental import pallas as pl
from jax.experimental.pallas import tpu as pltpu
from jax.sharding import Mesh
from jax.sharding import PartitionSpec as P

STATE = 128
EPSILON = 1e-05
PROMPTS = 7
HEAD = 64
BLOCK = 128
ZS, XS, HS = 16, 4, 8
ROW = 512
BLOCKS = ROW // BLOCK
WIDTH = 256
WIDE = 512
STEPS, SENT = 64, 72
FEW = 2
REQUEST = 96
BIG = 1 << 30
F32 = jnp.float32
BF16 = jnp.bfloat16


def dot(a, b, dims, precision=None):
    return lax.dot_general(a, b, (dims, ((), ())), precision=precision, preferred_element_type=F32)


def bounds(length_ref):
    starts, ends = [], []
    total = jnp.int32(0)
    for p in range(PROMPTS):
        starts.append(total)
        total = total + length_ref[p]
        ends.append(total - 1)
    return starts, ends


def segment_at(position, starts):
    found = jnp.zeros_like(position) - 1
    for start in starts:
        found = found + (position >= start).astype(jnp.int32)
    return found


def iota(shape, axis):
    return lax.broadcasted_iota(jnp.int32, shape, axis)


def spread(weights, tile, lane):
    left = jnp.broadcast_to(weights[:, 2 * tile : 2 * tile + 1], lane.shape)
    right = jnp.broadcast_to(weights[:, 2 * tile + 1 : 2 * tile + 2], lane.shape)
    return jnp.where(lane < HEAD, left, right)


def laid_out(value, at, lane):
    value = jnp.where(lane < 4, value, 0.0)
    first = value.astype(BF16).astype(F32)
    second = (value - first).astype(BF16).astype(F32)
    third = value - first - second
    out = jnp.zeros_like(value)
    for k, part in enumerate((first, second, third)):
        shift = at + 4 * k
        out = out + (pltpu.roll(part, shift, 1) if shift else part)
    return out


def picks(head, at):
    lane = iota((128, 128), 0)
    return ((lane == at + head) | (lane == at + 4 + head) | (lane == at + 8 + head)).astype(BF16)


def pack_kernel(request_ref, inner_ref, proj_ref, step_ref, out_ref):
    step = step_ref[...].astype(F32)
    lane = iota((8, 128), 1)
    request = request_ref[0, 0].astype(F32)
    for q in range(XS):
        for h in range(HS):
            at = q * HS + h
            for c in range(2):
                col = h * 1024 + q * WIDTH + c * 128
                out_ref[at, c * 16 : c * 16 + 16, :] = inner_ref[:, col : col + 128]
                col = h * 256 + c * 128
                out_ref[at, 32 + c * 16 : 48 + c * 16, :] = proj_ref[:, col : col + 128]
            shift = (128 - (16 * h + 4 * q)) % 128
            early = pltpu.roll(step[0:8], shift, 1) if shift else step[0:8]
            shift = (shift + 64) % 128
            late = pltpu.roll(step[8:16], shift, 1) if shift else step[8:16]
            own = jnp.where(lane < 64, early, late)
            out_ref[at, STEPS:SENT, :] = jnp.where(lane == 4, request, own).astype(BF16)


def gate_kernel(gate_ref, out_ref):
    for h in range(HS):
        out_ref[h] = gate_ref[:, h * 1024 : (h + 1) * 1024]


def block_of(rows_ref, b, row):
    return rows_ref[8 * b : 8 * b + 8, row : row + 16, :].reshape(BLOCK, 128)


def steps_of(rows_ref, b):
    early = rows_ref[8 * b : 8 * b + 8, STEPS:SENT, :].astype(F32)
    late = pltpu.roll(early.reshape(64, 128), 64, 1).reshape(8, 8, 128)
    return jnp.concatenate([early, late], axis=1).reshape(BLOCK, 128)


def padded_rows(rows_ref, halo_ref, padded):
    for tile in range(WIDE // 128):
        cols = slice(tile * 128, (tile + 1) * 128)
        padded[0:8, cols] = halo_ref[tile].astype(F32)
        for b in range(BLOCKS):
            at = 8 + b * BLOCK
            padded[at : at + BLOCK, cols] = block_of(rows_ref, b, tile * 16).astype(F32)


def weigh(weighted, act_ref, decay_ref, step_ref, end_decay, member_of):
    lane = iota((BLOCK, 128), 1)
    for b in range(BLOCKS):
        rows = slice(b * BLOCK, (b + 1) * BLOCK)
        gap = jnp.minimum(end_decay - decay_ref[rows, :], 0.0)
        weights = jnp.where(member_of(b), jnp.exp(gap), 0.0) * step_ref[rows, :]
        for tile in range(2):
            cols = slice(tile * 128, (tile + 1) * 128)
            weighted[rows, cols] = (spread(weights, tile, lane) * act_ref[rows, cols].astype(F32)).astype(BF16)


def send_state(message_ref, at, weighted, act_ref):
    for tile in range(2):
        state = dot(weighted[:, tile * 128 : (tile + 1) * 128], act_ref[:, WIDTH : WIDTH + STATE], ((0,), (0,)))
        message_ref[tile * 8 : (tile + 1) * 8, at : at + 16, :] = state.astype(BF16).reshape(8, 16, 128)


def send_ends(slots, first, length_ref, rows_ref, act_ref, decay_ref, step_ref, message_ref, padded, weighted):
    starts, ends = bounds(length_ref)
    before = segment_at(first - 1, starts)
    last = segment_at(first + ROW - 1, starts)
    sub = iota((BLOCK, 128), 0)
    row = iota((1, 128), 1)
    index = iota((8, 128), 0)
    found = [[jnp.int32(BIG), jnp.int32(-2), jnp.int32(0)] for _ in range(slots)]
    count = jnp.int32(0)
    for p in range(PROMPTS):
        here = (ends[p] >= first) & (ends[p] < first + ROW)
        for m in range(slots):
            mine = here & (count == m)
            for at, value in enumerate((ends[p], jnp.int32(p), starts[p])):
                found[m][at] = jnp.where(mine, value, found[m][at])
        count = count + here.astype(jnp.int32)
    carry = decay_ref[ROW - 1 : ROW, :]
    small = laid_out(jnp.where(last == before, jnp.exp(carry), 0.0), 0, row)
    edges = []
    for m in range(slots):
        end, prompt, start = found[m]
        some = end < BIG
        local = jnp.where(some, end - first, 0)
        end_decay = decay_ref[pl.ds(local, 1), :]
        at = 16 * (m + 1)

        @pl.when(some)
        def _(end=end, start=start, end_decay=end_decay, at=at):
            def member_of(b):
                position = sub + (first + b * BLOCK)
                return (position >= start) & (position <= end)

            weigh(weighted, act_ref, decay_ref, step_ref, end_decay, member_of)
            send_state(message_ref, at, weighted, act_ref)

        @pl.when(jnp.logical_not(some))
        def _(at=at):
            message_ref[:, at : at + 16, :] = jnp.zeros((ZS, 16, 128), BF16)

        carried = jnp.where(some & (prompt == before), jnp.exp(end_decay), 0.0)
        small = small + laid_out(carried, 12 * (m + 1), row)
        edge = []
        for k in range(3):
            valid = some & (end - 2 + k >= start)
            edge.append(jnp.where(valid, padded[pl.ds(8 + local - 2 + k, 1), :], 0.0))
        edges.append(edge)
    for k in range(XS):
        request = rows_ref[k * 8, STEPS:SENT, :].astype(F32)[0:1, :]
        small = small + jnp.where(row == REQUEST + k, pltpu.roll(request, REQUEST - 4 + k, 1), 0.0)
    block = jnp.where(index == slots, small, jnp.zeros((8, 128), F32))
    tail = 16 * (slots + 1)
    for k in range(ZS):
        value = block
        if k < 12:
            for m in range(slots):
                piece = edges[m][k // 4][:, (k % 4) * 128 : (k % 4 + 1) * 128]
                value = jnp.where(index == m, piece, value)
        message_ref[k, tail : tail + 8, :] = value.astype(BF16)


def front_kernel(
    place_ref, length_ref, rows_ref, halo_ref, inner_taps_ref, state_taps_ref, head_ref,
    message_ref, act_ref, decay_ref, step_ref, padded, weighted,
):
    first = place_ref[0] * ROW
    quarter = place_ref[1]
    starts, _ = bounds(length_ref)
    sub = iota((BLOCK, 128), 0)
    last = segment_at(first + ROW - 1, starts)
    heads = pltpu.roll(head_ref[...], place_ref[2], 1)
    bias = heads[0:1, :]
    scale = -jnp.exp(heads[1:2, :])
    lower = (sub >= iota((BLOCK, 128), 1)).astype(F32)

    padded_rows(rows_ref, halo_ref, padded)
    carry = jnp.zeros((1, 128), F32)
    for b in range(BLOCKS):
        rows = slice(b * BLOCK, (b + 1) * BLOCK)
        position = sub + (first + b * BLOCK)
        row_start = jnp.zeros_like(position)
        for start in starts:
            row_start = jnp.where(position >= start, start, row_start)
        inside = [(position - 3 + k) >= row_start for k in range(4)]
        for tile in range(WIDE // 128):
            cols = slice(tile * 128, (tile + 1) * 128)
            total = jnp.zeros((BLOCK, 128), F32)
            for k in range(4):
                if tile < 2:
                    at = pl.multiple_of(quarter * WIDTH + tile * 128, 128)
                    taps = inner_taps_ref[k : k + 1, pl.ds(at, 128)]
                else:
                    taps = state_taps_ref[k : k + 1, (tile - 2) * 128 : (tile - 1) * 128]
                at = b * BLOCK + 5 + k
                total = total + jnp.where(inside[k], padded[at : at + BLOCK, cols], 0.0) * taps
            act_ref[rows, cols] = (total * jax.nn.sigmoid(total)).astype(BF16)
        step = jax.nn.softplus(steps_of(rows_ref, b) + bias)
        decay = dot(lower, step * scale, ((1,), (0,)), lax.Precision.HIGHEST) + carry
        carry = decay[BLOCK - 1 : BLOCK, :]
        step_ref[rows, :] = step
        decay_ref[rows, :] = decay

    def member_of(b):
        return segment_at(sub + (first + b * BLOCK), starts) == last

    weigh(weighted, act_ref, decay_ref, step_ref, carry, member_of)
    send_state(message_ref, 0, weighted, act_ref)
    send_ends(FEW, first, length_ref, rows_ref, act_ref, decay_ref, step_ref, message_ref, padded, weighted)


def many_kernel(
    place_ref, length_ref, rows_ref, halo_ref, act_ref, decay_ref, step_ref, few_ref, message_ref, padded, weighted,
):
    padded_rows(rows_ref, halo_ref, padded)
    message_ref[:, 0:16, :] = few_ref[:, 0:16, :]
    send_ends(
        PROMPTS, place_ref[0] * ROW, length_ref, rows_ref, act_ref, decay_ref, step_ref, message_ref, padded, weighted
    )


def scan_kernel(slots, place_ref, length_ref, got_ref, out_ref, small, states, finals):
    _, ends = bounds(length_ref)
    head = place_ref[0] // 4
    tail_at = 16 * (slots + 1)
    one = [picks(head, 12 * m) for m in range(slots + 1)]
    one = one + [(iota((128, 128), 0) == REQUEST + k).astype(BF16) for k in range(XS)]
    small[...] = dot(got_ref[:, tail_at : tail_at + 8, :].reshape(ZS * 8, 128), jnp.concatenate(one, axis=1), ((1,), (0,)))
    state = jnp.zeros((16, 128), F32)
    for j in range(ZS):
        states[j] = state
        out_ref[j, 0:16, :] = state.astype(BF16)
        at = 8 * j + slots
        state = small[at : at + 1, 0:128] * state + got_ref[j, 0:16, :].astype(F32)
    for p in range(PROMPTS):
        z = ends[p] // ROW
        rank = jnp.int32(0)
        for other in range(p):
            rank = rank + (ends[other] // ROW == z).astype(jnp.int32)
        value = jnp.zeros((24, 128), F32)
        state = states[z]
        tail = got_ref[z, tail_at : tail_at + 8, :].astype(F32)
        factor = small[pl.ds(8 * z + slots, 1), 128 : 128 * (slots + 1)]
        for m in range(slots):
            own = got_ref[z, 16 * m + 16 : 16 * m + 32, :].astype(F32) + factor[:, 128 * m : 128 * (m + 1)] * state
            edge = jnp.broadcast_to(tail[m : m + 1, :], (8, 128))
            value = jnp.where(rank == m, jnp.concatenate([own, edge], axis=0), value)
        finals[p] = value
    index = iota((8, 128), 0)
    for z in range(ZS):
        edges = jnp.zeros((8, 128), F32)
        for k in range(XS):
            at = 128 * (slots + 1 + k)
            request = small[8 * z + slots : 8 * z + slots + 1, at : at + 128]
            value = finals[0]
            for p in range(1, PROMPTS):
                value = jnp.where(request == float(p), finals[p], value)
            out_ref[z, 16 * k + 16 : 16 * k + 32, :] = value[0:16].astype(BF16)
            edges = jnp.where(index == k, value[16:24], edges)
        out_ref[z, 80:88, :] = edges.astype(BF16)


def within_kernel(
    place_ref, length_ref, act_ref, decay_ref, step_ref, skip_ref, own_ref, in_ref, carried,
):
    first = place_ref[0] * ROW
    quarter = place_ref[1]
    starts, _ = bounds(length_ref)
    before_row = segment_at(first - 1, starts)
    lane = iota((BLOCK, 128), 1)
    sub = iota((BLOCK, 128), 0)
    carry = jnp.zeros((1, 128), F32)
    for b in range(BLOCKS):
        rows = slice(b * BLOCK, (b + 1) * BLOCK)
        at = first + b * BLOCK
        before = segment_at(at - 1, starts)
        last = segment_at(at + BLOCK - 1, starts)
        segment = segment_at(sub + at, starts)
        causal = (segment == segment_at(lane + at, starts)) & (sub >= lane)
        write = act_ref[rows, WIDTH : WIDTH + STATE]
        read = act_ref[rows, WIDTH + STATE : WIDE]
        scores = dot(read, write, ((1,), (1,)))
        decay = decay_ref[rows, :]
        step = step_ref[rows, :]
        decay_t = decay.T
        step_t = step.T
        inflow = jnp.where(segment == before, jnp.exp(jnp.minimum(decay - carry, 0.0)), 0.0)
        inflow_row = jnp.where(segment == before_row, jnp.exp(decay), 0.0)
        end = decay[BLOCK - 1 : BLOCK, :]
        tail = jnp.where(segment == last, jnp.exp(jnp.minimum(end - decay, 0.0)), 0.0) * step
        keep = jnp.where(last == before, jnp.exp(end - carry), 0.0)
        for tile in range(2):
            cols = slice(tile * 128, (tile + 1) * 128)
            x = act_ref[rows, cols]
            mixing = []
            for head in (2 * tile, 2 * tile + 1):
                gap = decay[:, head : head + 1] - decay_t[head : head + 1, :]
                weight = jnp.exp(jnp.where(causal, gap, -jnp.inf))
                mixing.append((scores * weight * step_t[head : head + 1, :]).astype(BF16))
            none = jnp.zeros_like(x)
            both = jnp.concatenate([jnp.where(lane < HEAD, x, none), jnp.where(lane < HEAD, none, x)], axis=0)
            value = dot(jnp.concatenate(mixing, axis=1), both, ((1,), (0,)))
            skip = skip_ref[0:1, pl.ds(pl.multiple_of(quarter * WIDTH + tile * 128, 128), 128)]
            value = value + skip * x.astype(F32)
            if b:
                across = dot(read.astype(F32), carried[tile], ((1,), (1,)), lax.Precision.HIGHEST)
                value = value + spread(inflow, tile, lane) * across
            own_ref[rows, cols] = value
            in_ref[rows, cols] = spread(inflow_row, tile, lane)
            if b < BLOCKS - 1:
                weighted = (spread(tail, tile, lane) * x.astype(F32)).astype(BF16)
                state = dot(weighted, write, ((0,), (0,)))
                if b:
                    factor = jnp.where(sub < HEAD, keep[:, 2 * tile : 2 * tile + 1], keep[:, 2 * tile + 1 : 2 * tile + 2])
                    state = factor * carried[tile] + state
                carried[tile] = state
        carry = end


def across_kernel(act_ref, own_ref, in_ref, got_ref, out_ref):
    for tile in range(2):
        cols = slice(tile * 128, (tile + 1) * 128)
        state = got_ref[tile * 8 : (tile + 1) * 8, 0:16, :].reshape(128, 128)
        for b in range(BLOCKS):
            rows = slice(b * BLOCK, (b + 1) * BLOCK)
            across = dot(act_ref[rows, WIDTH + STATE : WIDE], state, ((1,), (1,)))
            value = own_ref[rows, cols] + in_ref[rows, cols] * across
            out_ref[b, tile * BLOCK : (tile + 1) * BLOCK, :] = value.astype(BF16)
    index = iota((16, 128), 0)
    edges = [jnp.zeros((16, 128), F32) for _ in range(XS)]
    for i in range(ZS):
        tail = got_ref[i, 80:88, :].astype(F32)
        for k in range(XS):
            at = 2 * BLOCK + 16 * i
            out_ref[k, at : at + 16, :] = got_ref[i, 16 * k + 16 : 16 * k + 32, :]
            if i < 12:
                edges[k] = jnp.where(index == i, tail[k : k + 1, :], edges[k])
    for k in range(XS):
        out_ref[k, 512:528, :] = edges[k].astype(BF16)


def last_kernel(got_ref, gate_ref, gain_ref, hidden_ref, final_ref, inner_ref, proj_ref, gated):
    total = jnp.zeros((BLOCK, 128), F32)
    for q in range(XS):
        for tile in range(2):
            cols = slice(q * WIDTH + tile * 128, q * WIDTH + (tile + 1) * 128)
            gate = gate_ref[:, cols].astype(F32)
            value = got_ref[q, tile * BLOCK : (tile + 1) * BLOCK, :].astype(F32) * (gate * jax.nn.sigmoid(gate))
            gated[:, cols] = value
            total = total + value * value
    mean = jnp.sum(total, axis=1, keepdims=True) * (1.0 / (XS * WIDTH))
    inverse = lax.rsqrt(mean + EPSILON)
    for q in range(XS):
        for tile in range(2):
            cols = slice(q * WIDTH + tile * 128, q * WIDTH + (tile + 1) * 128)
            hidden_ref[:, cols] = ((gated[:, cols] * inverse) * gain_ref[:, cols]).astype(BF16)
        final_ref[q * WIDTH : (q + 1) * WIDTH, :] = got_ref[q, 256:512, :].astype(F32)
        edges = got_ref[q, 512:528, :].astype(F32)
        for k in range(3):
            for c in range(2):
                at = q * WIDTH + c * 128
                inner_ref[0, k : k + 1, at : at + 128] = edges[4 * k + c : 4 * k + c + 1, :].astype(BF16)
                if q == 0:
                    proj_ref[0, k : k + 1, c * 128 : (c + 1) * 128] = edges[4 * k + 2 + c : 4 * k + 3 + c, :].astype(BF16)


def call(kernel, ins, outs, scratch=(), scalars=0, limit=24 << 20):
    smem = pl.BlockSpec(memory_space=pltpu.SMEM)
    vmem = pl.BlockSpec(memory_space=pltpu.VMEM)
    return pl.pallas_call(
        kernel,
        out_shape=outs,
        in_specs=[smem] * scalars + [vmem] * (len(ins) - scalars),
        out_specs=jax.tree.map(lambda _: vmem, outs),
        scratch_shapes=list(scratch),
        compiler_params=pltpu.CompilerParams(vmem_limit_bytes=limit),
    )(*ins)


def swapped(blocks, bit, mask):
    keep = lax.dynamic_index_in_dim(blocks, bit, 2, keepdims=False)
    send = lax.dynamic_index_in_dim(blocks, 1 - bit, 2, keepdims=False)
    got = lax.ppermute(send, "head", [(source, source ^ mask) for source in range(HS)])
    return jnp.where(bit == 0, jnp.stack([keep, got]), jnp.stack([got, keep]))


def per_device(
    head_inputs,
    state_proj,
    gate_inputs,
    step_raw,
    step_bias,
    decay_log,
    skip_gain,
    filter_inner,
    filter_state,
    norm_gain,
    prompt_lengths,
    request_prompt,
):
    shape = jax.ShapeDtypeStruct
    place = lax.axis_index("z").astype(jnp.int32)
    quarter = lax.axis_index("x").astype(jnp.int32)
    heads = step_bias.shape[0]
    places = jnp.stack([place, quarter, (128 - 4 * quarter) % 128])
    heads_in = jnp.pad(jnp.stack([step_bias, decay_log]), ((0, 6), (0, 128 - heads)))
    skip = jnp.repeat(skip_gain, HEAD)[None]
    packed = call(
        pack_kernel,
        (request_prompt, head_inputs, state_proj, step_raw),
        shape((XS * HS, SENT, 128), BF16),
        scalars=1,
        limit=None,
    )
    head = lax.axis_index("head").astype(jnp.int32)
    rows = lax.all_to_all(packed, ("x", "head"), 0, 0)
    gate = call(gate_kernel, (gate_inputs,), shape((HS, 16, XS * WIDTH), BF16))
    gate = gate.reshape(2, 2, 2, 16, XS * WIDTH)
    gate = swapped(gate, head & 1, 1)
    gate = swapped(gate, (head >> 1) & 1, 2)
    gate = swapped(gate, head >> 2, 4)
    halo = lax.ppermute(rows[-1, :STEPS].reshape(WIDE // 128, 16, 128)[:, 8:], "z", [(source, source + 1) for source in range(ZS - 1)])
    message, act, decay, step = call(
        front_kernel,
        (places, prompt_lengths, rows, halo, filter_inner, filter_state, heads_in),
        (
            shape((ZS, 16 * (FEW + 1) + 8, 128), BF16),
            shape((ROW, WIDE), BF16),
            shape((ROW, 128), F32),
            shape((ROW, 128), F32),
        ),
        (pltpu.VMEM((ROW + 8, WIDE), F32), pltpu.VMEM((ROW, WIDTH), BF16)),
        scalars=2,
    )
    scratch = (pltpu.VMEM((ROW + 8, WIDE), F32), pltpu.VMEM((ROW, WIDTH), BF16))

    def onward(slots, message):
        got = lax.all_to_all(message, "z", 0, 0)
        own, inflow = call(
            within_kernel,
            (places, prompt_lengths, act, decay, step, skip),
            (shape((ROW, WIDTH), F32), shape((ROW, WIDTH), F32)),
            (pltpu.VMEM((2, 128, 128), F32),),
            scalars=2,
        )
        answer = call(
            functools.partial(scan_kernel, slots),
            (places, prompt_lengths, got),
            shape((ZS, 88, 128), BF16),
            (
                pltpu.VMEM((ZS * 8, 128 * (slots + 1 + XS)), F32),
                pltpu.VMEM((ZS, 16, 128), F32),
                pltpu.VMEM((PROMPTS, 24, 128), F32),
            ),
            scalars=2,
        )
        return answer, own, inflow

    def many():
        full = call(
            many_kernel,
            (places, prompt_lengths, rows, halo, act, decay, step, message),
            shape((ZS, 16 * (PROMPTS + 1) + 8, 128), BF16),
            scratch,
            scalars=2,
        )
        return onward(PROMPTS, full)

    z = (jnp.cumsum(prompt_lengths) - 1) // ROW
    most = jnp.max(jnp.sum((z[None, :] == z[:, None]).astype(jnp.int32), axis=1))
    answer, own, inflow = lax.cond(most > FEW, many, lambda: onward(FEW, message))
    back = lax.all_to_all(answer, "z", 0, 0)
    shared = call(across_kernel, (act, own, inflow, back), shape((XS, 528, 128), BF16))
    shared = lax.all_to_all(shared, "x", 0, 0)
    hidden, final, edge_inner, edge_state = call(
        last_kernel,
        (shared, gate.reshape(BLOCK, XS * WIDTH), norm_gain[None]),
        (
            shape((BLOCK, XS * WIDTH), BF16),
            shape((XS * WIDTH, STATE), F32),
            shape((1, 3, XS * WIDTH), BF16),
            shape((1, 3, 256), BF16),
        ),
        (pltpu.VMEM((BLOCK, XS * WIDTH), F32),),
    )
    return hidden, final.reshape(1, heads, HEAD, STATE), edge_inner, edge_state


def solution(mesh):
    seq = ("z", "x")
    mesh = Mesh(mesh.devices.reshape(ZS, XS, HS), ("z", "x", "head"))
    tokens = P(("z", "x", "head"), None)
    return jax.shard_map(
        per_device,
        mesh=mesh,
        in_specs=(
            tokens,
            tokens,
            tokens,
            tokens,
            P("head"),
            P("head"),
            P("head"),
            P(None, "head"),
            P(None, "head"),
            P("head"),
            P(),
            P(seq, None),
        ),
        out_specs=(
            P(seq, "head"),
            P(seq, "head", None, None),
            P(seq, None, "head"),
            P(seq, None, "head"),
        ),
        check_vma=False,
    )
```

```python
import functools

import jax
import jax.numpy as jnp
from jax import lax
from jax.experimental import pallas as pl
from jax.experimental.pallas import tpu as pltpu
from jax.sharding import Mesh
from jax.sharding import PartitionSpec as P

STATE = 128
EPSILON = 1e-05
PROMPTS = 7
HEAD = 64
BLOCK = 128
ZS, XS, HS = 16, 4, 8
ROW = 512
BLOCKS = ROW // BLOCK
WIDTH = 256
WIDE = 512
STEPS, SENT = 64, 72
FEW = 2
REQUEST = 96
BIG = 1 << 30
F32 = jnp.float32
BF16 = jnp.bfloat16


def dot(a, b, dims, precision=None):
    return lax.dot_general(a, b, (dims, ((), ())), precision=precision, preferred_element_type=F32)


def bounds(length_ref):
    starts, ends = [], []
    total = jnp.int32(0)
    for p in range(PROMPTS):
        starts.append(total)
        total = total + length_ref[p]
        ends.append(total - 1)
    return starts, ends


def segment_at(position, starts):
    found = jnp.zeros_like(position) - 1
    for start in starts:
        found = found + (position >= start).astype(jnp.int32)
    return found


def iota(shape, axis):
    return lax.broadcasted_iota(jnp.int32, shape, axis)


def spread(weights, tile, lane):
    left = jnp.broadcast_to(weights[:, 2 * tile : 2 * tile + 1], lane.shape)
    right = jnp.broadcast_to(weights[:, 2 * tile + 1 : 2 * tile + 2], lane.shape)
    return jnp.where(lane < HEAD, left, right)


def laid_out(value, at, lane):
    value = jnp.where(lane < 4, value, 0.0)
    first = value.astype(BF16).astype(F32)
    second = (value - first).astype(BF16).astype(F32)
    third = value - first - second
    out = jnp.zeros_like(value)
    for k, part in enumerate((first, second, third)):
        shift = at + 4 * k
        out = out + (pltpu.roll(part, shift, 1) if shift else part)
    return out


def picks(head, at):
    lane = iota((128, 128), 0)
    return ((lane == at + head) | (lane == at + 4 + head) | (lane == at + 8 + head)).astype(BF16)


def pack_kernel(request_ref, inner_ref, proj_ref, step_ref, out_ref):
    step = step_ref[...].astype(F32)
    lane = iota((8, 128), 1)
    request = request_ref[0, 0].astype(F32)
    for q in range(XS):
        for h in range(HS):
            at = q * HS + h
            for c in range(2):
                col = h * 1024 + q * WIDTH + c * 128
                out_ref[at, c * 16 : c * 16 + 16, :] = inner_ref[:, col : col + 128]
                col = h * 256 + c * 128
                out_ref[at, 32 + c * 16 : 48 + c * 16, :] = proj_ref[:, col : col + 128]
            shift = (128 - (16 * h + 4 * q)) % 128
            early = pltpu.roll(step[0:8], shift, 1) if shift else step[0:8]
            shift = (shift + 64) % 128
            late = pltpu.roll(step[8:16], shift, 1) if shift else step[8:16]
            own = jnp.where(lane < 64, early, late)
            out_ref[at, STEPS:SENT, :] = jnp.where(lane == 4, request, own).astype(BF16)


def gate_kernel(gate_ref, out_ref):
    for h in range(HS):
        out_ref[h] = gate_ref[:, h * 1024 : (h + 1) * 1024]


def block_of(rows_ref, b, row):
    return rows_ref[8 * b : 8 * b + 8, row : row + 16, :].reshape(BLOCK, 128)


def steps_of(rows_ref, b):
    early = rows_ref[8 * b : 8 * b + 8, STEPS:SENT, :].astype(F32)
    late = pltpu.roll(early.reshape(64, 128), 64, 1).reshape(8, 8, 128)
    return jnp.concatenate([early, late], axis=1).reshape(BLOCK, 128)


def tokens(act, b):
    return (act[0], slice(0, BLOCK)) if b == 0 else (act[1], slice((b - 1) * BLOCK, b * BLOCK))


def convolve(out_ref, out_at, padded, at, b, first, starts, taps_ref):
    position = iota((BLOCK, 128), 0) + (first + b * BLOCK)
    row_start = jnp.zeros_like(position)
    for start in starts:
        row_start = jnp.where(position >= start, start, row_start)
    inside = [(position - 3 + k) >= row_start for k in range(4)]
    for tile in range(WIDE // 128):
        cols = slice(tile * 128, (tile + 1) * 128)
        total = jnp.zeros((BLOCK, 128), F32)
        for k in range(4):
            total = total + jnp.where(inside[k], padded[at - 3 + k : at - 3 + k + BLOCK, cols], 0.0) * taps_ref[k : k + 1, cols]
        out_ref[out_at : out_at + BLOCK, cols] = (total * jax.nn.sigmoid(total)).astype(BF16)


def outer(weighted, act, blocks, decay_ref, step_ref, end_decay, member_of):
    lane = iota((BLOCK, 128), 1)
    for at, b in enumerate(blocks):
        rows = slice(b * BLOCK, (b + 1) * BLOCK)
        ref, held = tokens(act, b)
        gap = jnp.minimum(end_decay - decay_ref[rows, :], 0.0)
        weights = jnp.where(member_of(b), jnp.exp(gap), 0.0) * step_ref[rows, :]
        for tile in range(2):
            cols = slice(tile * 128, (tile + 1) * 128)
            value = spread(weights, tile, lane) * ref[held, cols].astype(F32)
            weighted[at * BLOCK : (at + 1) * BLOCK, cols] = value.astype(BF16)
    out = []
    for tile in range(2):
        cols = slice(tile * 128, (tile + 1) * 128)
        total, at = None, 0
        for ref, count in ((act[0], int(0 in blocks)), (act[1], len([b for b in blocks if b]))):
            if count:
                part = dot(weighted[at * BLOCK : (at + count) * BLOCK, cols], ref[:, WIDTH : WIDTH + STATE], ((0,), (0,)))
                total = part if total is None else total + part
                at += count
        out.append(total)
    return out


def send_state(message_ref, at, state):
    for tile in range(2):
        message_ref[tile * 8 : (tile + 1) * 8, at : at + 16, :] = state[tile].astype(BF16).reshape(8, 16, 128)


def ends_in(slots, first, starts, ends):
    found = [[jnp.int32(BIG), jnp.int32(-2), jnp.int32(0)] for _ in range(slots)]
    count = jnp.int32(0)
    for p in range(PROMPTS):
        here = (ends[p] >= first) & (ends[p] < first + ROW)
        for m in range(slots):
            mine = here & (count == m)
            for at, value in enumerate((ends[p], jnp.int32(p), starts[p])):
                found[m][at] = jnp.where(mine, value, found[m][at])
        count = count + here.astype(jnp.int32)
    return found


def between(first, start, end):
    def member_of(b):
        position = iota((BLOCK, 128), 0) + (first + b * BLOCK)
        return (position >= start) & (position <= end)

    return member_of


def raw_row(rows_ref, halo_ref, local, tile):
    inside = jnp.maximum(local, 0)
    block = rows_ref[inside // 16, tile * 16 : tile * 16 + 16, :].astype(F32)
    here = jnp.sum(jnp.where(iota((16, 128), 0) == inside % 16, block, 0.0), axis=0, keepdims=True)
    before = jnp.sum(jnp.where(iota((8, 128), 0) == local + 8, halo_ref[tile].astype(F32), 0.0), axis=0, keepdims=True)
    return jnp.where(local >= 0, here, before)


def send_ends(
    slots, first, length_ref, rows_ref, halo_ref, act, blocks, decay_ref, step_ref, part_ref, message_ref, weighted,
):
    starts, ends = bounds(length_ref)
    before = segment_at(first - 1, starts)
    last = segment_at(first + ROW - 1, starts)
    row = iota((1, 128), 1)
    index = iota((8, 128), 0)
    carry = decay_ref[ROW - 1 : ROW, :]
    small = laid_out(jnp.where(last == before, jnp.exp(carry), 0.0), 0, row)
    edges = []
    for m, (end, prompt, start) in enumerate(ends_in(slots, first, starts, ends)):
        some = end < BIG
        local = jnp.where(some, end - first, 0)
        end_decay = decay_ref[pl.ds(local, 1), :]
        at = 16 * (m + 1)

        @pl.when(some)
        def _(end=end, start=start, end_decay=end_decay, at=at, m=m):
            state = outer(weighted, act, blocks, decay_ref, step_ref, end_decay, between(first, start, end))
            if part_ref is not None:
                state = [state[tile] + part_ref[m + 1, tile] for tile in range(2)]
            send_state(message_ref, at, state)

        @pl.when(jnp.logical_not(some))
        def _(at=at):
            message_ref[:, at : at + 16, :] = jnp.zeros((ZS, 16, 128), BF16)

        carried = jnp.where(some & (prompt == before), jnp.exp(end_decay), 0.0)
        small = small + laid_out(carried, 12 * (m + 1), row)
        edge = []
        for k in range(3):
            valid = some & (end - 2 + k >= start)
            edge.append([jnp.where(valid, raw_row(rows_ref, halo_ref, local - 2 + k, tile), 0.0) for tile in range(4)])
        edges.append(edge)
    for k in range(XS):
        request = rows_ref[k * 8, STEPS:SENT, :].astype(F32)[0:1, :]
        small = small + jnp.where(row == REQUEST + k, pltpu.roll(request, REQUEST - 4 + k, 1), 0.0)
    block = jnp.where(index == slots, small, jnp.zeros((8, 128), F32))
    tail = 16 * (slots + 1)
    for k in range(ZS):
        value = block
        if k < 12:
            for m in range(slots):
                value = jnp.where(index == m, edges[m][k // 4][k % 4], value)
        message_ref[k, tail : tail + 8, :] = value.astype(BF16)


def taps_kernel(place_ref, inner_ref, state_ref, out_ref):
    for tile in range(2):
        cols = slice(tile * 128, (tile + 1) * 128)
        out_ref[:, cols] = inner_ref[:, pl.ds(pl.multiple_of(place_ref[1] * WIDTH + tile * 128, 128), 128)]
    out_ref[:, WIDTH:] = state_ref[...]


def early_kernel(
    place_ref, length_ref, rows_ref, taps_ref, head_ref,
    rest_ref, decay_ref, step_ref, part_ref, padded, weighted,
):
    first = place_ref[0] * ROW
    starts, ends = bounds(length_ref)
    sub = iota((BLOCK, 128), 0)
    last = segment_at(first + ROW - 1, starts)
    heads = pltpu.roll(head_ref[...], place_ref[2], 1)
    bias = heads[0:1, :]
    scale = -jnp.exp(heads[1:2, :])
    lower = (sub >= iota((BLOCK, 128), 1)).astype(F32)
    for tile in range(WIDE // 128):
        cols = slice(tile * 128, (tile + 1) * 128)
        padded[0:8, cols] = rows_ref[7, tile * 16 : tile * 16 + 16, :].astype(F32)[8:16]
        for b in range(1, BLOCKS):
            at = 8 + (b - 1) * BLOCK
            padded[at : at + BLOCK, cols] = block_of(rows_ref, b, tile * 16).astype(F32)
    carry = jnp.zeros((1, 128), F32)
    for b in range(BLOCKS):
        rows = slice(b * BLOCK, (b + 1) * BLOCK)
        step = jax.nn.softplus(steps_of(rows_ref, b) + bias)
        decay = dot(lower, step * scale, ((1,), (0,)), lax.Precision.HIGHEST) + carry
        carry = decay[BLOCK - 1 : BLOCK, :]
        step_ref[rows, :] = step
        decay_ref[rows, :] = decay
        if b:
            at = (b - 1) * BLOCK
            convolve(rest_ref, at, padded, at + 8, b, first, starts, taps_ref)

    def member_of(b):
        return segment_at(sub + (first + b * BLOCK), starts) == last

    act, blocks = (None, rest_ref), (1, 2, 3)
    state = outer(weighted, act, blocks, decay_ref, step_ref, carry, member_of)
    part_ref[0, 0], part_ref[0, 1] = state
    for m, (end, _, start) in enumerate(ends_in(FEW, first, starts, ends)):

        @pl.when(end < BIG)
        def _(end=end, start=start, m=m):
            end_decay = decay_ref[pl.ds(end - first, 1), :]
            state = outer(weighted, act, blocks, decay_ref, step_ref, end_decay, between(first, start, end))
            part_ref[m + 1, 0], part_ref[m + 1, 1] = state


def front_kernel(
    place_ref, length_ref, rows_ref, halo_ref, taps_ref, decay_ref, step_ref, part_ref,
    message_ref, act_ref, padded, weighted,
):
    first = place_ref[0] * ROW
    starts, _ = bounds(length_ref)
    sub = iota((BLOCK, 128), 0)
    last = segment_at(first + ROW - 1, starts)
    for tile in range(WIDE // 128):
        cols = slice(tile * 128, (tile + 1) * 128)
        padded[0:8, cols] = halo_ref[tile].astype(F32)
        padded[8:, cols] = block_of(rows_ref, 0, tile * 16).astype(F32)
    convolve(act_ref, 0, padded, 8, 0, first, starts, taps_ref)

    def member_of(b):
        return segment_at(sub + (first + b * BLOCK), starts) == last

    act, blocks = (act_ref, None), (0,)
    state = outer(weighted, act, blocks, decay_ref, step_ref, decay_ref[ROW - 1 : ROW, :], member_of)
    send_state(message_ref, 0, [state[tile] + part_ref[0, tile] for tile in range(2)])
    send_ends(
        FEW, first, length_ref, rows_ref, halo_ref, act, blocks, decay_ref, step_ref, part_ref, message_ref, weighted
    )


def many_kernel(
    place_ref, length_ref, rows_ref, halo_ref, act_ref, rest_ref, decay_ref, step_ref, few_ref, message_ref, weighted,
):
    message_ref[:, 0:16, :] = few_ref[:, 0:16, :]
    send_ends(
        PROMPTS, place_ref[0] * ROW, length_ref, rows_ref, halo_ref, (act_ref, rest_ref), (0, 1, 2, 3),
        decay_ref, step_ref, None, message_ref, weighted,
    )


def scan_kernel(slots, place_ref, length_ref, got_ref, out_ref, small, states, finals):
    _, ends = bounds(length_ref)
    head = place_ref[0] // 4
    tail_at = 16 * (slots + 1)
    one = [picks(head, 12 * m) for m in range(slots + 1)]
    one = one + [(iota((128, 128), 0) == REQUEST + k).astype(BF16) for k in range(XS)]
    small[...] = dot(got_ref[:, tail_at : tail_at + 8, :].reshape(ZS * 8, 128), jnp.concatenate(one, axis=1), ((1,), (0,)))
    state = jnp.zeros((16, 128), F32)
    for j in range(ZS):
        states[j] = state
        out_ref[j, 0:16, :] = state.astype(BF16)
        at = 8 * j + slots
        state = small[at : at + 1, 0:128] * state + got_ref[j, 0:16, :].astype(F32)
    for p in range(PROMPTS):
        z = ends[p] // ROW
        rank = jnp.int32(0)
        for other in range(p):
            rank = rank + (ends[other] // ROW == z).astype(jnp.int32)
        value = jnp.zeros((24, 128), F32)
        state = states[z]
        tail = got_ref[z, tail_at : tail_at + 8, :].astype(F32)
        factor = small[pl.ds(8 * z + slots, 1), 128 : 128 * (slots + 1)]
        for m in range(slots):
            own = got_ref[z, 16 * m + 16 : 16 * m + 32, :].astype(F32) + factor[:, 128 * m : 128 * (m + 1)] * state
            edge = jnp.broadcast_to(tail[m : m + 1, :], (8, 128))
            value = jnp.where(rank == m, jnp.concatenate([own, edge], axis=0), value)
        finals[p] = value
    index = iota((8, 128), 0)
    for z in range(ZS):
        edges = jnp.zeros((8, 128), F32)
        for k in range(XS):
            at = 128 * (slots + 1 + k)
            request = small[8 * z + slots : 8 * z + slots + 1, at : at + 128]
            value = finals[0]
            for p in range(1, PROMPTS):
                value = jnp.where(request == float(p), finals[p], value)
            out_ref[z, 16 * k + 16 : 16 * k + 32, :] = value[0:16].astype(BF16)
            edges = jnp.where(index == k, value[16:24], edges)
        out_ref[z, 80:88, :] = edges.astype(BF16)


def within_kernel(
    place_ref, length_ref, act_ref, rest_ref, decay_ref, step_ref, skip_ref, own_ref, in_ref, carried,
):
    first = place_ref[0] * ROW
    quarter = place_ref[1]
    starts, _ = bounds(length_ref)
    before_row = segment_at(first - 1, starts)
    lane = iota((BLOCK, 128), 1)
    sub = iota((BLOCK, 128), 0)
    carry = jnp.zeros((1, 128), F32)
    for b in range(BLOCKS):
        rows = slice(b * BLOCK, (b + 1) * BLOCK)
        at = first + b * BLOCK
        before = segment_at(at - 1, starts)
        last = segment_at(at + BLOCK - 1, starts)
        segment = segment_at(sub + at, starts)
        causal = (segment == segment_at(lane + at, starts)) & (sub >= lane)
        ref, held = tokens((act_ref, rest_ref), b)
        write = ref[held, WIDTH : WIDTH + STATE]
        read = ref[held, WIDTH + STATE : WIDE]
        scores = dot(read, write, ((1,), (1,)))
        decay = decay_ref[rows, :]
        step = step_ref[rows, :]
        decay_t = decay.T
        step_t = step.T
        inflow = jnp.where(segment == before, jnp.exp(jnp.minimum(decay - carry, 0.0)), 0.0)
        inflow_row = jnp.where(segment == before_row, jnp.exp(decay), 0.0)
        end = decay[BLOCK - 1 : BLOCK, :]
        tail = jnp.where(segment == last, jnp.exp(jnp.minimum(end - decay, 0.0)), 0.0) * step
        keep = jnp.where(last == before, jnp.exp(end - carry), 0.0)
        for tile in range(2):
            cols = slice(tile * 128, (tile + 1) * 128)
            x = ref[held, cols]
            mixing = []
            for head in (2 * tile, 2 * tile + 1):
                gap = decay[:, head : head + 1] - decay_t[head : head + 1, :]
                weight = jnp.exp(jnp.where(causal, gap, -jnp.inf))
                mixing.append((scores * weight * step_t[head : head + 1, :]).astype(BF16))
            none = jnp.zeros_like(x)
            both = jnp.concatenate([jnp.where(lane < HEAD, x, none), jnp.where(lane < HEAD, none, x)], axis=0)
            value = dot(jnp.concatenate(mixing, axis=1), both, ((1,), (0,)))
            skip = skip_ref[0:1, pl.ds(pl.multiple_of(quarter * WIDTH + tile * 128, 128), 128)]
            value = value + skip * x.astype(F32)
            if b:
                across = dot(read.astype(F32), carried[tile], ((1,), (1,)), lax.Precision.HIGHEST)
                value = value + spread(inflow, tile, lane) * across
            own_ref[rows, cols] = value
            in_ref[rows, cols] = spread(inflow_row, tile, lane)
            if b < BLOCKS - 1:
                weighted = (spread(tail, tile, lane) * x.astype(F32)).astype(BF16)
                state = dot(weighted, write, ((0,), (0,)))
                if b:
                    factor = jnp.where(sub < HEAD, keep[:, 2 * tile : 2 * tile + 1], keep[:, 2 * tile + 1 : 2 * tile + 2])
                    state = factor * carried[tile] + state
                carried[tile] = state
        carry = end


def across_kernel(act_ref, rest_ref, own_ref, in_ref, got_ref, out_ref):
    for tile in range(2):
        cols = slice(tile * 128, (tile + 1) * 128)
        state = got_ref[tile * 8 : (tile + 1) * 8, 0:16, :].reshape(128, 128)
        for b in range(BLOCKS):
            rows = slice(b * BLOCK, (b + 1) * BLOCK)
            ref, held = tokens((act_ref, rest_ref), b)
            across = dot(ref[held, WIDTH + STATE : WIDE], state, ((1,), (1,)))
            value = own_ref[rows, cols] + in_ref[rows, cols] * across
            out_ref[b, tile * BLOCK : (tile + 1) * BLOCK, :] = value.astype(BF16)
    index = iota((16, 128), 0)
    edges = [jnp.zeros((16, 128), F32) for _ in range(XS)]
    for i in range(ZS):
        tail = got_ref[i, 80:88, :].astype(F32)
        for k in range(XS):
            at = 2 * BLOCK + 16 * i
            out_ref[k, at : at + 16, :] = got_ref[i, 16 * k + 16 : 16 * k + 32, :]
            if i < 12:
                edges[k] = jnp.where(index == i, tail[k : k + 1, :], edges[k])
    for k in range(XS):
        out_ref[k, 512:528, :] = edges[k].astype(BF16)


def last_kernel(got_ref, gate_ref, gain_ref, hidden_ref, final_ref, inner_ref, proj_ref, gated):
    total = jnp.zeros((BLOCK, 128), F32)
    for q in range(XS):
        for tile in range(2):
            cols = slice(q * WIDTH + tile * 128, q * WIDTH + (tile + 1) * 128)
            gate = gate_ref[:, cols].astype(F32)
            value = got_ref[q, tile * BLOCK : (tile + 1) * BLOCK, :].astype(F32) * (gate * jax.nn.sigmoid(gate))
            gated[:, cols] = value
            total = total + value * value
    mean = jnp.sum(total, axis=1, keepdims=True) * (1.0 / (XS * WIDTH))
    inverse = lax.rsqrt(mean + EPSILON)
    for q in range(XS):
        for tile in range(2):
            cols = slice(q * WIDTH + tile * 128, q * WIDTH + (tile + 1) * 128)
            hidden_ref[:, cols] = ((gated[:, cols] * inverse) * gain_ref[:, cols]).astype(BF16)
        final_ref[q * WIDTH : (q + 1) * WIDTH, :] = got_ref[q, 256:512, :].astype(F32)
        edges = got_ref[q, 512:528, :].astype(F32)
        for k in range(3):
            for c in range(2):
                at = q * WIDTH + c * 128
                inner_ref[0, k : k + 1, at : at + 128] = edges[4 * k + c : 4 * k + c + 1, :].astype(BF16)
                if q == 0:
                    proj_ref[0, k : k + 1, c * 128 : (c + 1) * 128] = edges[4 * k + 2 + c : 4 * k + 3 + c, :].astype(BF16)


def call(kernel, ins, outs, scratch=(), scalars=0, limit=24 << 20):
    smem = pl.BlockSpec(memory_space=pltpu.SMEM)
    vmem = pl.BlockSpec(memory_space=pltpu.VMEM)
    return pl.pallas_call(
        kernel,
        out_shape=outs,
        in_specs=[smem] * scalars + [vmem] * (len(ins) - scalars),
        out_specs=jax.tree.map(lambda _: vmem, outs),
        scratch_shapes=list(scratch),
        compiler_params=pltpu.CompilerParams(vmem_limit_bytes=limit),
    )(*ins)


def swapped(blocks, bit, mask):
    keep = lax.dynamic_index_in_dim(blocks, bit, 2, keepdims=False)
    send = lax.dynamic_index_in_dim(blocks, 1 - bit, 2, keepdims=False)
    got = lax.ppermute(send, "head", [(source, source ^ mask) for source in range(HS)])
    return jnp.where(bit == 0, jnp.stack([keep, got]), jnp.stack([got, keep]))


def per_device(
    head_inputs,
    state_proj,
    gate_inputs,
    step_raw,
    step_bias,
    decay_log,
    skip_gain,
    filter_inner,
    filter_state,
    norm_gain,
    prompt_lengths,
    request_prompt,
):
    shape = jax.ShapeDtypeStruct
    place = lax.axis_index("z").astype(jnp.int32)
    quarter = lax.axis_index("x").astype(jnp.int32)
    heads = step_bias.shape[0]
    places = jnp.stack([place, quarter, (128 - 4 * quarter) % 128])
    packed = call(
        pack_kernel,
        (request_prompt, head_inputs, state_proj, step_raw),
        shape((XS * HS, SENT, 128), BF16),
        scalars=1,
        limit=None,
    )
    head = lax.axis_index("head").astype(jnp.int32)
    rows = lax.all_to_all(packed, ("x", "head"), 0, 0)
    gate = call(gate_kernel, (gate_inputs,), shape((HS, 16, XS * WIDTH), BF16))
    gate = gate.reshape(2, 2, 2, 16, XS * WIDTH)
    taps = call(taps_kernel, (places, filter_inner, filter_state), shape((4, WIDE), F32), scalars=1)
    heads_in = jnp.pad(jnp.stack([step_bias, decay_log]), ((0, 6), (0, 128 - heads)))
    skip = jnp.repeat(skip_gain, HEAD)[None]
    z = (jnp.cumsum(prompt_lengths) - 1) // ROW
    most = jnp.max(jnp.sum((z[None, :] == z[:, None]).astype(jnp.int32), axis=1))
    crowded = most > FEW
    gate = swapped(gate, head & 1, 1)
    gate = swapped(gate, (head >> 1) & 1, 2)
    gate = swapped(gate, head >> 2, 4)
    halo = lax.ppermute(
        rows[-1, :STEPS].reshape(WIDE // 128, 16, 128)[:, 8:],
        "z",
        [(source, source + 1) for source in range(ZS - 1)],
    )
    weighted = pltpu.VMEM((ROW, WIDTH), BF16)
    rest, decay, step, part = call(
        early_kernel,
        (places, prompt_lengths, rows, taps, heads_in),
        (
            shape((ROW - BLOCK, WIDE), BF16),
            shape((ROW, 128), F32),
            shape((ROW, 128), F32),
            shape((FEW + 1, 2, 128, 128), F32),
        ),
        (pltpu.VMEM((ROW - BLOCK + 8, WIDE), F32), weighted),
        scalars=2,
    )
    message, act = call(
        front_kernel,
        (places, prompt_lengths, rows, halo, taps, decay, step, part),
        (shape((ZS, 16 * (FEW + 1) + 8, 128), BF16), shape((BLOCK, WIDE), BF16)),
        (pltpu.VMEM((BLOCK + 8, WIDE), F32), weighted),
        scalars=2,
    )

    def onward(slots, message):
        got = lax.all_to_all(message, "z", 0, 0)
        own, inflow = call(
            within_kernel,
            (places, prompt_lengths, act, rest, decay, step, skip),
            (shape((ROW, WIDTH), F32), shape((ROW, WIDTH), F32)),
            (pltpu.VMEM((2, 128, 128), F32),),
            scalars=2,
        )
        answer = call(
            functools.partial(scan_kernel, slots),
            (places, prompt_lengths, got),
            shape((ZS, 88, 128), BF16),
            (
                pltpu.VMEM((ZS * 8, 128 * (slots + 1 + XS)), F32),
                pltpu.VMEM((ZS, 16, 128), F32),
                pltpu.VMEM((PROMPTS, 24, 128), F32),
            ),
            scalars=2,
        )
        return answer, own, inflow

    def many():
        full = call(
            many_kernel,
            (places, prompt_lengths, rows, halo, act, rest, decay, step, message),
            shape((ZS, 16 * (PROMPTS + 1) + 8, 128), BF16),
            (weighted,),
            scalars=2,
        )
        return onward(PROMPTS, full)

    answer, own, inflow = lax.cond(crowded, many, lambda: onward(FEW, message))
    back = lax.all_to_all(answer, "z", 0, 0)
    shared = call(across_kernel, (act, rest, own, inflow, back), shape((XS, 528, 128), BF16))
    shared = lax.all_to_all(shared, "x", 0, 0)
    hidden, final, edge_inner, edge_state = call(
        last_kernel,
        (shared, gate.reshape(BLOCK, XS * WIDTH), norm_gain[None]),
        (
            shape((BLOCK, XS * WIDTH), BF16),
            shape((XS * WIDTH, STATE), F32),
            shape((1, 3, XS * WIDTH), BF16),
            shape((1, 3, 256), BF16),
        ),
        (pltpu.VMEM((BLOCK, XS * WIDTH), F32),),
    )
    return hidden, final.reshape(1, heads, HEAD, STATE), edge_inner, edge_state


def solution(mesh):
    seq = ("z", "x")
    mesh = Mesh(mesh.devices.reshape(ZS, XS, HS), ("z", "x", "head"))
    tokens = P(("z", "x", "head"), None)
    return jax.shard_map(
        per_device,
        mesh=mesh,
        in_specs=(
            tokens,
            tokens,
            tokens,
            tokens,
            P("head"),
            P("head"),
            P("head"),
            P(None, "head"),
            P(None, "head"),
            P("head"),
            P(),
            P(seq, None),
        ),
        out_specs=(
            P(seq, "head"),
            P(seq, "head", None, None),
            P(seq, None, "head"),
            P(seq, None, "head"),
        ),
        check_vma=False,
    )
```

```python
import functools

import jax
import jax.numpy as jnp
from jax import lax
from jax.experimental import pallas as pl
from jax.experimental.pallas import tpu as pltpu
from jax.sharding import Mesh
from jax.sharding import PartitionSpec as P

STATE = 128
EPSILON = 1e-05
PROMPTS = 7
HEAD = 64
BLOCK = 128
ZS, XS, HS = 16, 4, 8
ROW = 512
BLOCKS = ROW // BLOCK
WIDTH = 256
WIDE = 512
STEPS, SENT = 64, 72
FEW = 2
REQUEST = 96
BIG = 1 << 30
F32 = jnp.float32
BF16 = jnp.bfloat16


def dot(a, b, dims, precision=None):
    return lax.dot_general(a, b, (dims, ((), ())), precision=precision, preferred_element_type=F32)


def bounds(length_ref):
    starts, ends = [], []
    total = jnp.int32(0)
    for p in range(PROMPTS):
        starts.append(total)
        total = total + length_ref[p]
        ends.append(total - 1)
    return starts, ends


def segment_at(position, starts):
    found = jnp.zeros_like(position) - 1
    for start in starts:
        found = found + (position >= start).astype(jnp.int32)
    return found


def iota(shape, axis):
    return lax.broadcasted_iota(jnp.int32, shape, axis)


def spread(weights, tile, lane):
    left = jnp.broadcast_to(weights[:, 2 * tile : 2 * tile + 1], lane.shape)
    right = jnp.broadcast_to(weights[:, 2 * tile + 1 : 2 * tile + 2], lane.shape)
    return jnp.where(lane < HEAD, left, right)


def laid_out(value, at, lane):
    value = jnp.where(lane < 4, value, 0.0)
    first = value.astype(BF16).astype(F32)
    second = (value - first).astype(BF16).astype(F32)
    third = value - first - second
    out = jnp.zeros_like(value)
    for k, part in enumerate((first, second, third)):
        shift = at + 4 * k
        out = out + (pltpu.roll(part, shift, 1) if shift else part)
    return out


def picks(head, at):
    lane = iota((128, 128), 0)
    return ((lane == at + head) | (lane == at + 4 + head) | (lane == at + 8 + head)).astype(BF16)


def pack_kernel(request_ref, inner_ref, proj_ref, step_ref, out_ref):
    step = step_ref[...].astype(F32)
    lane = iota((8, 128), 1)
    request = request_ref[0, 0].astype(F32)
    for q in range(XS):
        for h in range(HS):
            at = q * HS + h
            for c in range(2):
                col = h * 1024 + q * WIDTH + c * 128
                out_ref[at, c * 16 : c * 16 + 16, :] = inner_ref[:, col : col + 128]
                col = h * 256 + c * 128
                out_ref[at, 32 + c * 16 : 48 + c * 16, :] = proj_ref[:, col : col + 128]
            shift = (128 - (16 * h + 4 * q)) % 128
            early = pltpu.roll(step[0:8], shift, 1) if shift else step[0:8]
            shift = (shift + 64) % 128
            late = pltpu.roll(step[8:16], shift, 1) if shift else step[8:16]
            own = jnp.where(lane < 64, early, late)
            out_ref[at, STEPS:SENT, :] = jnp.where(lane == 4, request, own).astype(BF16)


def gate_kernel(gate_ref, out_ref):
    for h in range(HS):
        out_ref[h] = gate_ref[:, h * 1024 : (h + 1) * 1024]


def block_of(rows_ref, b, row):
    return rows_ref[8 * b : 8 * b + 8, row : row + 16, :].reshape(BLOCK, 128)


def steps_of(rows_ref, b):
    early = rows_ref[8 * b : 8 * b + 8, STEPS:SENT, :].astype(F32)
    late = pltpu.roll(early.reshape(64, 128), 64, 1).reshape(8, 8, 128)
    return jnp.concatenate([early, late], axis=1).reshape(BLOCK, 128)


def tokens(act, b):
    return (act[0], slice(0, BLOCK)) if b == 0 else (act[1], slice((b - 1) * BLOCK, b * BLOCK))


def convolve(out_ref, out_at, padded, at, b, first, starts, taps_ref):
    position = iota((BLOCK, 128), 0) + (first + b * BLOCK)
    row_start = jnp.zeros_like(position)
    for start in starts:
        row_start = jnp.where(position >= start, start, row_start)
    inside = [(position - 3 + k) >= row_start for k in range(4)]
    for tile in range(WIDE // 128):
        cols = slice(tile * 128, (tile + 1) * 128)
        total = jnp.zeros((BLOCK, 128), F32)
        for k in range(4):
            total = total + jnp.where(inside[k], padded[at - 3 + k : at - 3 + k + BLOCK, cols], 0.0) * taps_ref[k : k + 1, cols]
        out_ref[out_at : out_at + BLOCK, cols] = (total * jax.nn.sigmoid(total)).astype(BF16)


def outer(weighted, act, blocks, decay_ref, step_ref, end_decay, member_of):
    lane = iota((BLOCK, 128), 1)
    for at, b in enumerate(blocks):
        rows = slice(b * BLOCK, (b + 1) * BLOCK)
        ref, held = tokens(act, b)
        gap = jnp.minimum(end_decay - decay_ref[rows, :], 0.0)
        weights = jnp.where(member_of(b), jnp.exp(gap), 0.0) * step_ref[rows, :]
        for tile in range(2):
            cols = slice(tile * 128, (tile + 1) * 128)
            value = spread(weights, tile, lane) * ref[held, cols].astype(F32)
            weighted[at * BLOCK : (at + 1) * BLOCK, cols] = value.astype(BF16)
    out = []
    for tile in range(2):
        cols = slice(tile * 128, (tile + 1) * 128)
        total, at = None, 0
        for ref, count in ((act[0], int(0 in blocks)), (act[1], len([b for b in blocks if b]))):
            if count:
                part = dot(weighted[at * BLOCK : (at + count) * BLOCK, cols], ref[:, WIDTH : WIDTH + STATE], ((0,), (0,)))
                total = part if total is None else total + part
                at += count
        out.append(total)
    return out


def send_state(message_ref, at, state):
    for tile in range(2):
        message_ref[tile * 8 : (tile + 1) * 8, at : at + 16, :] = state[tile].astype(BF16).reshape(8, 16, 128)


def ends_in(slots, first, starts, ends):
    found = [[jnp.int32(BIG), jnp.int32(-2), jnp.int32(0)] for _ in range(slots)]
    count = jnp.int32(0)
    for p in range(PROMPTS):
        here = (ends[p] >= first) & (ends[p] < first + ROW)
        for m in range(slots):
            mine = here & (count == m)
            for at, value in enumerate((ends[p], jnp.int32(p), starts[p])):
                found[m][at] = jnp.where(mine, value, found[m][at])
        count = count + here.astype(jnp.int32)
    return found


def between(first, start, end):
    def member_of(b):
        position = iota((BLOCK, 128), 0) + (first + b * BLOCK)
        return (position >= start) & (position <= end)

    return member_of


def raw_row(rows_ref, halo_ref, local, tile):
    inside = jnp.maximum(local, 0)
    block = rows_ref[inside // 16, tile * 16 : tile * 16 + 16, :].astype(F32)
    here = jnp.sum(jnp.where(iota((16, 128), 0) == inside % 16, block, 0.0), axis=0, keepdims=True)
    before = jnp.sum(jnp.where(iota((8, 128), 0) == local + 8, halo_ref[tile].astype(F32), 0.0), axis=0, keepdims=True)
    return jnp.where(local >= 0, here, before)


def send_ends(
    slots, first, length_ref, rows_ref, halo_ref, act, blocks, decay_ref, step_ref, part_ref, message_ref, weighted,
):
    starts, ends = bounds(length_ref)
    before = segment_at(first - 1, starts)
    last = segment_at(first + ROW - 1, starts)
    row = iota((1, 128), 1)
    index = iota((8, 128), 0)
    carry = decay_ref[ROW - 1 : ROW, :]
    small = laid_out(jnp.where(last == before, jnp.exp(carry), 0.0), 0, row)
    edges = []
    for m, (end, prompt, start) in enumerate(ends_in(slots, first, starts, ends)):
        some = end < BIG
        local = jnp.where(some, end - first, 0)
        end_decay = decay_ref[pl.ds(local, 1), :]
        at = 16 * (m + 1)

        @pl.when(some)
        def _(end=end, start=start, end_decay=end_decay, at=at, m=m):
            state = outer(weighted, act, blocks, decay_ref, step_ref, end_decay, between(first, start, end))
            if part_ref is not None:
                state = [state[tile] + part_ref[m + 1, tile] for tile in range(2)]
            send_state(message_ref, at, state)

        @pl.when(jnp.logical_not(some))
        def _(at=at):
            message_ref[:, at : at + 16, :] = jnp.zeros((ZS, 16, 128), BF16)

        carried = jnp.where(some & (prompt == before), jnp.exp(end_decay), 0.0)
        small = small + laid_out(carried, 12 * (m + 1), row)
        edge = []
        for k in range(3):
            valid = some & (end - 2 + k >= start)
            edge.append([jnp.where(valid, raw_row(rows_ref, halo_ref, local - 2 + k, tile), 0.0) for tile in range(4)])
        edges.append(edge)
    for k in range(XS):
        request = rows_ref[k * 8, STEPS:SENT, :].astype(F32)[0:1, :]
        small = small + jnp.where(row == REQUEST + k, pltpu.roll(request, REQUEST - 4 + k, 1), 0.0)
    block = jnp.where(index == slots, small, jnp.zeros((8, 128), F32))
    tail = 16 * (slots + 1)
    for k in range(ZS):
        value = block
        if k < 12:
            for m in range(slots):
                value = jnp.where(index == m, edges[m][k // 4][k % 4], value)
        message_ref[k, tail : tail + 8, :] = value.astype(BF16)


def taps_kernel(place_ref, inner_ref, state_ref, out_ref):
    for tile in range(2):
        cols = slice(tile * 128, (tile + 1) * 128)
        out_ref[:, cols] = inner_ref[:, pl.ds(pl.multiple_of(place_ref[1] * WIDTH + tile * 128, 128), 128)]
    out_ref[:, WIDTH:] = state_ref[...]


def early_kernel(
    place_ref, length_ref, rows_ref, taps_ref, head_ref,
    rest_ref, decay_ref, step_ref, part_ref, padded, weighted,
):
    first = place_ref[0] * ROW
    starts, ends = bounds(length_ref)
    sub = iota((BLOCK, 128), 0)
    last = segment_at(first + ROW - 1, starts)
    heads = pltpu.roll(head_ref[...], place_ref[2], 1)
    bias = heads[0:1, :]
    scale = -jnp.exp(heads[1:2, :])
    lower = (sub >= iota((BLOCK, 128), 1)).astype(F32)
    for tile in range(WIDE // 128):
        cols = slice(tile * 128, (tile + 1) * 128)
        padded[0:8, cols] = rows_ref[7, tile * 16 : tile * 16 + 16, :].astype(F32)[8:16]
        for b in range(1, BLOCKS):
            at = 8 + (b - 1) * BLOCK
            padded[at : at + BLOCK, cols] = block_of(rows_ref, b, tile * 16).astype(F32)
    carry = jnp.zeros((1, 128), F32)
    for b in range(BLOCKS):
        rows = slice(b * BLOCK, (b + 1) * BLOCK)
        step = jax.nn.softplus(steps_of(rows_ref, b) + bias)
        decay = dot(lower, step * scale, ((1,), (0,)), lax.Precision.HIGHEST) + carry
        carry = decay[BLOCK - 1 : BLOCK, :]
        step_ref[rows, :] = step
        decay_ref[rows, :] = decay
        if b:
            at = (b - 1) * BLOCK
            convolve(rest_ref, at, padded, at + 8, b, first, starts, taps_ref)

    def member_of(b):
        return segment_at(sub + (first + b * BLOCK), starts) == last

    act, blocks = (None, rest_ref), (1, 2, 3)
    state = outer(weighted, act, blocks, decay_ref, step_ref, carry, member_of)
    part_ref[0, 0], part_ref[0, 1] = state
    for m, (end, _, start) in enumerate(ends_in(FEW, first, starts, ends)):

        @pl.when(end < BIG)
        def _(end=end, start=start, m=m):
            end_decay = decay_ref[pl.ds(end - first, 1), :]
            state = outer(weighted, act, blocks, decay_ref, step_ref, end_decay, between(first, start, end))
            part_ref[m + 1, 0], part_ref[m + 1, 1] = state


def front_kernel(
    place_ref, length_ref, rows_ref, halo_ref, taps_ref, decay_ref, step_ref, part_ref,
    message_ref, act_ref, padded, weighted,
):
    first = place_ref[0] * ROW
    starts, _ = bounds(length_ref)
    sub = iota((BLOCK, 128), 0)
    last = segment_at(first + ROW - 1, starts)
    for tile in range(WIDE // 128):
        cols = slice(tile * 128, (tile + 1) * 128)
        padded[0:8, cols] = halo_ref[tile].astype(F32)
        padded[8:, cols] = block_of(rows_ref, 0, tile * 16).astype(F32)
    convolve(act_ref, 0, padded, 8, 0, first, starts, taps_ref)

    def member_of(b):
        return segment_at(sub + (first + b * BLOCK), starts) == last

    act, blocks = (act_ref, None), (0,)
    state = outer(weighted, act, blocks, decay_ref, step_ref, decay_ref[ROW - 1 : ROW, :], member_of)
    send_state(message_ref, 0, [state[tile] + part_ref[0, tile] for tile in range(2)])
    send_ends(
        FEW, first, length_ref, rows_ref, halo_ref, act, blocks, decay_ref, step_ref, part_ref, message_ref, weighted
    )


def many_kernel(
    place_ref, length_ref, rows_ref, halo_ref, act_ref, rest_ref, decay_ref, step_ref, few_ref, message_ref, weighted,
):
    message_ref[:, 0:16, :] = few_ref[:, 0:16, :]
    send_ends(
        PROMPTS, place_ref[0] * ROW, length_ref, rows_ref, halo_ref, (act_ref, rest_ref), (0, 1, 2, 3),
        decay_ref, step_ref, None, message_ref, weighted,
    )


def scan_kernel(slots, place_ref, length_ref, got_ref, sent_ref, small, states, finals, out_ref, sems):
    _, ends = bounds(length_ref)
    head = place_ref[0] // 4
    tail_at = 16 * (slots + 1)
    one = [picks(head, 12 * m) for m in range(slots + 1)]
    one = one + [(iota((128, 128), 0) == REQUEST + k).astype(BF16) for k in range(XS)]
    small[...] = dot(got_ref[:, tail_at : tail_at + 8, :].reshape(ZS * 8, 128), jnp.concatenate(one, axis=1), ((1,), (0,)))
    state = jnp.zeros((16, 128), F32)
    for j in range(ZS):
        states[j] = state
        out_ref[j, 0:16, :] = state.astype(BF16)
        at = 8 * j + slots
        state = small[at : at + 1, 0:128] * state + got_ref[j, 0:16, :].astype(F32)
    for p in range(PROMPTS):
        z = ends[p] // ROW
        rank = jnp.int32(0)
        for other in range(p):
            rank = rank + (ends[other] // ROW == z).astype(jnp.int32)
        value = jnp.zeros((24, 128), F32)
        state = states[z]
        tail = got_ref[z, tail_at : tail_at + 8, :].astype(F32)
        factor = small[pl.ds(8 * z + slots, 1), 128 : 128 * (slots + 1)]
        for m in range(slots):
            own = got_ref[z, 16 * m + 16 : 16 * m + 32, :].astype(F32) + factor[:, 128 * m : 128 * (m + 1)] * state
            edge = jnp.broadcast_to(tail[m : m + 1, :], (8, 128))
            value = jnp.where(rank == m, jnp.concatenate([own, edge], axis=0), value)
        finals[p] = value
    index = iota((8, 128), 0)
    copies = []
    for z in range(ZS):
        edges = jnp.zeros((8, 128), F32)
        for k in range(XS):
            at = 128 * (slots + 1 + k)
            request = small[8 * z + slots : 8 * z + slots + 1, at : at + 128]
            value = finals[0]
            for p in range(1, PROMPTS):
                value = jnp.where(request == float(p), finals[p], value)
            out_ref[z, 16 * k + 16 : 16 * k + 32, :] = value[0:16].astype(BF16)
            edges = jnp.where(index == k, value[16:24], edges)
        out_ref[z, 80:88, :] = edges.astype(BF16)
        copies.append(pltpu.make_async_copy(out_ref.at[z], sent_ref.at[z], sems.at[z]))
        copies[-1].start()
    for copy in copies:
        copy.wait()


def within_kernel(
    place_ref, length_ref, act_ref, rest_ref, decay_ref, step_ref, skip_ref, own_ref, in_ref, carried,
):
    first = place_ref[0] * ROW
    quarter = place_ref[1]
    starts, _ = bounds(length_ref)
    before_row = segment_at(first - 1, starts)
    lane = iota((BLOCK, 128), 1)
    sub = iota((BLOCK, 128), 0)
    carry = jnp.zeros((1, 128), F32)
    for b in range(BLOCKS):
        rows = slice(b * BLOCK, (b + 1) * BLOCK)
        at = first + b * BLOCK
        before = segment_at(at - 1, starts)
        last = segment_at(at + BLOCK - 1, starts)
        segment = segment_at(sub + at, starts)
        causal = (segment == segment_at(lane + at, starts)) & (sub >= lane)
        ref, held = tokens((act_ref, rest_ref), b)
        write = ref[held, WIDTH : WIDTH + STATE]
        read = ref[held, WIDTH + STATE : WIDE]
        scores = dot(read, write, ((1,), (1,)))
        decay = decay_ref[rows, :]
        step = step_ref[rows, :]
        decay_t = decay.T
        step_t = step.T
        inflow = jnp.where(segment == before, jnp.exp(jnp.minimum(decay - carry, 0.0)), 0.0)
        inflow_row = jnp.where(segment == before_row, jnp.exp(decay), 0.0)
        end = decay[BLOCK - 1 : BLOCK, :]
        tail = jnp.where(segment == last, jnp.exp(jnp.minimum(end - decay, 0.0)), 0.0) * step
        keep = jnp.where(last == before, jnp.exp(end - carry), 0.0)
        for tile in range(2):
            cols = slice(tile * 128, (tile + 1) * 128)
            x = ref[held, cols]
            mixing = []
            for head in (2 * tile, 2 * tile + 1):
                gap = decay[:, head : head + 1] - decay_t[head : head + 1, :]
                weight = jnp.exp(jnp.where(causal, gap, -jnp.inf))
                mixing.append((scores * weight * step_t[head : head + 1, :]).astype(BF16))
            none = jnp.zeros_like(x)
            both = jnp.concatenate([jnp.where(lane < HEAD, x, none), jnp.where(lane < HEAD, none, x)], axis=0)
            value = dot(jnp.concatenate(mixing, axis=1), both, ((1,), (0,)))
            skip = skip_ref[0:1, pl.ds(pl.multiple_of(quarter * WIDTH + tile * 128, 128), 128)]
            value = value + skip * x.astype(F32)
            if b:
                across = dot(read.astype(F32), carried[tile], ((1,), (1,)), lax.Precision.HIGHEST)
                value = value + spread(inflow, tile, lane) * across
            own_ref[rows, cols] = value
            in_ref[rows, cols] = spread(inflow_row, tile, lane)
            if b < BLOCKS - 1:
                weighted = (spread(tail, tile, lane) * x.astype(F32)).astype(BF16)
                state = dot(weighted, write, ((0,), (0,)))
                if b:
                    factor = jnp.where(sub < HEAD, keep[:, 2 * tile : 2 * tile + 1], keep[:, 2 * tile + 1 : 2 * tile + 2])
                    state = factor * carried[tile] + state
                carried[tile] = state
        carry = end


def across_kernel(act_ref, rest_ref, own_ref, in_ref, got_ref, out_ref):
    for tile in range(2):
        cols = slice(tile * 128, (tile + 1) * 128)
        state = got_ref[tile * 8 : (tile + 1) * 8, 0:16, :].reshape(128, 128)
        for b in range(BLOCKS):
            rows = slice(b * BLOCK, (b + 1) * BLOCK)
            ref, held = tokens((act_ref, rest_ref), b)
            across = dot(ref[held, WIDTH + STATE : WIDE], state, ((1,), (1,)))
            value = own_ref[rows, cols] + in_ref[rows, cols] * across
            out_ref[b, tile * BLOCK : (tile + 1) * BLOCK, :] = value.astype(BF16)
    index = iota((16, 128), 0)
    edges = [jnp.zeros((16, 128), F32) for _ in range(XS)]
    for i in range(ZS):
        tail = got_ref[i, 80:88, :].astype(F32)
        for k in range(XS):
            at = 2 * BLOCK + 16 * i
            out_ref[k, at : at + 16, :] = got_ref[i, 16 * k + 16 : 16 * k + 32, :]
            if i < 12:
                edges[k] = jnp.where(index == i, tail[k : k + 1, :], edges[k])
    for k in range(XS):
        out_ref[k, 512:528, :] = edges[k].astype(BF16)


def last_kernel(got_ref, gate_ref, gain_ref, hidden_ref, final_ref, inner_ref, proj_ref, gated):
    total = jnp.zeros((BLOCK, 128), F32)
    for q in range(XS):
        for tile in range(2):
            cols = slice(q * WIDTH + tile * 128, q * WIDTH + (tile + 1) * 128)
            gate = gate_ref[:, cols].astype(F32)
            value = got_ref[q, tile * BLOCK : (tile + 1) * BLOCK, :].astype(F32) * (gate * jax.nn.sigmoid(gate))
            gated[:, cols] = value
            total = total + value * value
    mean = jnp.sum(total, axis=1, keepdims=True) * (1.0 / (XS * WIDTH))
    inverse = lax.rsqrt(mean + EPSILON)
    for q in range(XS):
        for tile in range(2):
            cols = slice(q * WIDTH + tile * 128, q * WIDTH + (tile + 1) * 128)
            hidden_ref[:, cols] = ((gated[:, cols] * inverse) * gain_ref[:, cols]).astype(BF16)
        final_ref[q * WIDTH : (q + 1) * WIDTH, :] = got_ref[q, 256:512, :].astype(F32)
        edges = got_ref[q, 512:528, :].astype(F32)
        for k in range(3):
            for c in range(2):
                at = q * WIDTH + c * 128
                inner_ref[0, k : k + 1, at : at + 128] = edges[4 * k + c : 4 * k + c + 1, :].astype(BF16)
                if q == 0:
                    proj_ref[0, k : k + 1, c * 128 : (c + 1) * 128] = edges[4 * k + 2 + c : 4 * k + 3 + c, :].astype(BF16)


def call(kernel, ins, outs, scratch=(), scalars=0, limit=24 << 20, kept=False):
    smem = pl.BlockSpec(memory_space=pltpu.SMEM)
    vmem = pl.BlockSpec(memory_space=pltpu.VMEM)
    return pl.pallas_call(
        kernel,
        out_shape=outs,
        in_specs=[smem] * scalars + [vmem] * (len(ins) - scalars),
        out_specs=jax.tree.map(lambda _: pl.BlockSpec(memory_space=pl.ANY) if kept else vmem, outs),
        scratch_shapes=list(scratch),
        compiler_params=pltpu.CompilerParams(vmem_limit_bytes=limit),
    )(*ins)


def swapped(blocks, bit, mask):
    keep = lax.dynamic_index_in_dim(blocks, bit, 2, keepdims=False)
    send = lax.dynamic_index_in_dim(blocks, 1 - bit, 2, keepdims=False)
    got = lax.ppermute(send, "head", [(source, source ^ mask) for source in range(HS)])
    return jnp.where(bit == 0, jnp.stack([keep, got]), jnp.stack([got, keep]))


def per_device(
    head_inputs,
    state_proj,
    gate_inputs,
    step_raw,
    step_bias,
    decay_log,
    skip_gain,
    filter_inner,
    filter_state,
    norm_gain,
    prompt_lengths,
    request_prompt,
):
    shape = jax.ShapeDtypeStruct
    place = lax.axis_index("z").astype(jnp.int32)
    quarter = lax.axis_index("x").astype(jnp.int32)
    heads = step_bias.shape[0]
    places = jnp.stack([place, quarter, (128 - 4 * quarter) % 128])
    packed = call(
        pack_kernel,
        (request_prompt, head_inputs, state_proj, step_raw),
        shape((XS * HS, SENT, 128), BF16),
        scalars=1,
        limit=None,
    )
    head = lax.axis_index("head").astype(jnp.int32)
    rows = lax.all_to_all(packed, ("x", "head"), 0, 0)
    gate = call(gate_kernel, (gate_inputs,), shape((HS, 16, XS * WIDTH), BF16))
    gate = gate.reshape(2, 2, 2, 16, XS * WIDTH)
    taps = call(taps_kernel, (places, filter_inner, filter_state), shape((4, WIDE), F32), scalars=1)
    heads_in = jnp.pad(jnp.stack([step_bias, decay_log]), ((0, 6), (0, 128 - heads)))
    skip = jnp.repeat(skip_gain, HEAD)[None]
    z = (jnp.cumsum(prompt_lengths) - 1) // ROW
    most = jnp.max(jnp.sum((z[None, :] == z[:, None]).astype(jnp.int32), axis=1))
    crowded = most > FEW
    gate = swapped(gate, head & 1, 1)
    gate = swapped(gate, (head >> 1) & 1, 2)
    gate = swapped(gate, head >> 2, 4)
    halo = lax.ppermute(
        rows[-1, :STEPS].reshape(WIDE // 128, 16, 128)[:, 8:],
        "z",
        [(source, source + 1) for source in range(ZS - 1)],
    )
    weighted = pltpu.VMEM((ROW, WIDTH), BF16)
    rest, decay, step, part = call(
        early_kernel,
        (places, prompt_lengths, rows, taps, heads_in),
        (
            shape((ROW - BLOCK, WIDE), BF16),
            shape((ROW, 128), F32),
            shape((ROW, 128), F32),
            shape((FEW + 1, 2, 128, 128), F32),
        ),
        (pltpu.VMEM((ROW - BLOCK + 8, WIDE), F32), weighted),
        scalars=2,
    )
    message, act = call(
        front_kernel,
        (places, prompt_lengths, rows, halo, taps, decay, step, part),
        (shape((ZS, 16 * (FEW + 1) + 8, 128), BF16), shape((BLOCK, WIDE), BF16)),
        (pltpu.VMEM((BLOCK + 8, WIDE), F32), weighted),
        scalars=2,
    )

    def onward(slots, message):
        got = lax.all_to_all(message, "z", 0, 0)
        own, inflow = call(
            within_kernel,
            (places, prompt_lengths, act, rest, decay, step, skip),
            (shape((ROW, WIDTH), F32), shape((ROW, WIDTH), F32)),
            (pltpu.VMEM((2, 128, 128), F32),),
            scalars=2,
        )
        answer = call(
            functools.partial(scan_kernel, slots),
            (places, prompt_lengths, got),
            shape((ZS, 88, 128), BF16),
            (
                pltpu.VMEM((ZS * 8, 128 * (slots + 1 + XS)), F32),
                pltpu.VMEM((ZS, 16, 128), F32),
                pltpu.VMEM((PROMPTS, 24, 128), F32),
                pltpu.VMEM((ZS, 88, 128), BF16),
                pltpu.SemaphoreType.DMA((ZS,)),
            ),
            scalars=2,
            kept=True,
        )
        return answer, own, inflow

    def many():
        full = call(
            many_kernel,
            (places, prompt_lengths, rows, halo, act, rest, decay, step, message),
            shape((ZS, 16 * (PROMPTS + 1) + 8, 128), BF16),
            (weighted,),
            scalars=2,
        )
        return onward(PROMPTS, full)

    answer, own, inflow = lax.cond(crowded, many, lambda: onward(FEW, message))
    back = lax.all_to_all(answer, "z", 0, 0)
    shared = call(across_kernel, (act, rest, own, inflow, back), shape((XS, 528, 128), BF16))
    shared = lax.all_to_all(shared, "x", 0, 0)
    hidden, final, edge_inner, edge_state = call(
        last_kernel,
        (shared, gate.reshape(BLOCK, XS * WIDTH), norm_gain[None]),
        (
            shape((BLOCK, XS * WIDTH), BF16),
            shape((XS * WIDTH, STATE), F32),
            shape((1, 3, XS * WIDTH), BF16),
            shape((1, 3, 256), BF16),
        ),
        (pltpu.VMEM((BLOCK, XS * WIDTH), F32),),
    )
    return hidden, final.reshape(1, heads, HEAD, STATE), edge_inner, edge_state


def solution(mesh):
    seq = ("z", "x")
    mesh = Mesh(mesh.devices.reshape(ZS, XS, HS), ("z", "x", "head"))
    tokens = P(("z", "x", "head"), None)
    return jax.shard_map(
        per_device,
        mesh=mesh,
        in_specs=(
            tokens,
            tokens,
            tokens,
            tokens,
            P("head"),
            P("head"),
            P("head"),
            P(None, "head"),
            P(None, "head"),
            P("head"),
            P(),
            P(seq, None),
        ),
        out_specs=(
            P(seq, "head"),
            P(seq, "head", None, None),
            P(seq, None, "head"),
            P(seq, None, "head"),
        ),
        check_vma=False,
    )
```
